128 devices in a mesh: gx: 16 (over z, x_lo, core), gy: 8 (over x_hi, y).
Axes of the slice: x: 4 (x_hi: 2, x_lo: 2; x = x_hi * 2 + x_lo), y: 4, z: 4, core: 2. Of those that a mesh axis runs over, the one named last changes fastest.
Arguments:
- populations: float32 [19, 64, 256, 128], P(None, 'gx', 'gy'), may hold values from 0.5 to 1.5
- solid: int32 [64, 256, 128], P('gx', 'gy'), may hold values 0 or 1
- panel_cell: int32 [32768], P(('gx', 'gy')), may hold values from 0 to 16383
- panel_owner: int32 [32768], P(('gx', 'gy')), may hold values from 0 to 15, as said below
- panel_count: int32 [128], P(('gx', 'gy')), may hold values from 1 to 256, 16384 in all
- panel_area: float32 [3, 32768], P(None, ('gx', 'gy')), may hold values from -4 to 4
- observers: float32 [3, 256], replicated, may hold values from 0 to 288, as said below
- frequencies: float32 [64], replicated, may hold values from 0.01 to 1.5
Outputs:
- populations_out: float32 [19, 64, 256, 128], P(None, 'gx', 'gy')
- patch_spectra: float32 [16, 2, 64, 256], P('gx', None, 'gy')
The draws below stay inside these ranges and needn't reach their ends.
Inputs may be any that keep to these rules, and one draw needn't show every extreme that they name: `panel_owner`: among the 256 slots of each brick every patch is named by exactly 16 slots. `panel_count`: the counts of all bricks sum to 16384 and some brick has all 256 slots live. `observers`: every observer lies 16 or more cells above the lattice: its third coordinate is at least 144.
All inputs are finite; a program needn't handle non-finite values. No bound on the sum of `solid` on one device may be relied on, other than what follows from the above.
Results may differ from the reference program's by a relative error of at most 0.0003.
Values sent between devices are 32-bit elements; how exact they have to be, the bound alone decides.
No kernel may reach another device: no remote copies, remote signals or barrier semaphores. Data moves between devices by JAX's collectives and lax.ppermute only.
A program may use at most 64 MiB of HBM per device.

```python
import math
import jax
import jax.numpy as jnp
import numpy as np
from jax import lax

CX = 4
CY = 32
CZ = 128
STEPS = 4
LIST = 256
OBS = 256
FREQS = 64
NX = 64
NY = 256
PATCHES = 16
OWN_CAP = 16
N_GY = 8
DEVICES = 128


def draw_panel_owner(key, part):
    scores = jax.random.randint(key, (DEVICES, LIST), 0, 1 << 20) * LIST + jnp.arange(LIST, dtype=jnp.int32)[None, :]
    ordering = jnp.argsort(scores, axis=1)
    rank_table = jnp.argsort(ordering, axis=1)
    return (rank_table // OWN_CAP).astype(jnp.int32).reshape(DEVICES * LIST)


def draw_observers(key, part):
    key_a, key_b, key_c = jax.random.split(jax.random.fold_in(key, 7), 3)
    across_x = jax.random.uniform(key_a, (OBS,), jnp.float32) * NX
    across_y = jax.random.uniform(key_b, (OBS,), jnp.float32) * NY
    height = CZ + 32.0 + 128.0 * jax.random.uniform(key_c, (OBS,), jnp.float32)
    return jnp.stack([across_x, across_y, height]).astype(jnp.float32)


def set_ends(values, own_key, smallest, largest):
    dims = values.shape
    spot = [jax.random.randint(jax.random.fold_in(own_key, axis), (), 0, dims[axis]) for axis in range(len(dims))]
    values = values.at[tuple(spot)].set(smallest)
    longest = dims.index(max(dims))
    spot[longest] = (spot[longest] + 1) % dims[longest]
    return values.at[tuple(spot)].set(largest)


def steps_of(rng, dims, pieces, smallest, largest):
    factor_of, own = 1.0, jax.random.fold_in(rng, 6)
    for axis_at, parts in pieces:
        heights = jnp.exp(jax.random.uniform(jax.random.fold_in(own, axis_at), (parts,), jnp.float32, smallest / len(pieces), largest / len(pieces)))
        factor_of = factor_of * jnp.repeat(heights, dims[axis_at] // parts).reshape([-1 if axis == axis_at else 1 for axis in range(len(dims))])
    return factor_of


def length_profile(number_of, total, most, skew):
    portions = [(1 << 20) // math.isqrt(rank ** skew) + 1 for rank in range(2, number_of + 1)]
    rest, counts = total - most - (number_of - 1), [1] * (number_of - 1)
    while rest > 0:
        free = [i for i in range(number_of - 1) if counts[i] < most]
        mass, remaining = sum([portions[i] for i in free]), rest
        for i in free:
            extra = min(most - counts[i], max(1, remaining * portions[i] // mass), rest)
            counts[i] = counts[i] + extra
            rest = rest - extra
    return np.array([most] + counts)


def ragged_sizes(own_key, number_of, total, reach, slope):
    if number_of == 2:
        one = jax.random.randint(own_key, (), max(1, total - reach), min(reach, total - 1) + 1)
        return jnp.stack([one, total - one])
    tallies = jnp.asarray(length_profile(number_of, total, reach, slope), jnp.int32)
    pairs = (number_of - 1) // 2
    donor, receiver = tallies[1:1 + 2 * pairs:2], tallies[2:2 + 2 * pairs:2]
    room = jnp.minimum(donor - 1, reach - receiver)
    shifted = jax.random.randint(jax.random.fold_in(own_key, 1), (pairs,), 0, 1 << 20) % (room + 1)
    tallies = tallies.at[1:1 + 2 * pairs:2].set(donor - shifted).at[2:2 + 2 * pairs:2].set(receiver + shifted)
    return tallies[jax.random.permutation(jax.random.fold_in(own_key, 2), number_of)]


def bell_draw(own_key, dims, deviation, bound, pieces=(), held_as=jnp.bfloat16):
    drawn = deviation * jax.random.normal(own_key, dims, jnp.float32)
    if pieces:
        drawn = drawn * steps_of(own_key, dims, pieces, -0.22, 0.18)
    return jnp.clip(drawn, -bound, bound).astype(held_as)


def setup_inputs(seed: int = 0) -> dict:
    key_of = jax.random.split(jax.random.key(seed), 9)
    populations = jnp.clip(0.5 + 1.0 * jax.random.uniform(key_of[0], (19, NX, NY, CZ), jnp.float32) ** steps_of(key_of[0], (19, NX, NY, CZ), ((1, 16), (2, 8)), -0.2, 0.2), 0.5, 1.5)
    solid = set_ends((jax.random.randint(key_of[1], (NX, NY, CZ), 0, 8) < 1).astype(jnp.int32), jax.random.fold_in(key_of[1], 1), 0, 1)
    panel_cell = set_ends(jax.random.randint(key_of[2], (DEVICES * LIST,), 0, CX * CY * CZ), jax.random.fold_in(key_of[2], 1), 0, (CX * CY * CZ) - 1).astype(jnp.int32)
    panel_owner = draw_panel_owner(jax.random.fold_in(key_of[8], 71), 0)
    panel_count = ragged_sizes(key_of[4], DEVICES, DEVICES * LIST // 2, LIST, 2).astype(jnp.int32)
    panel_area = bell_draw(key_of[5], (3, DEVICES * LIST), 1.0, 4.0, ((1, 128),), jnp.float32)
    observers = draw_observers(jax.random.fold_in(key_of[8], 71), 0)
    frequencies = jnp.clip(jnp.exp(jax.random.uniform(key_of[7], (FREQS,), jnp.float32, math.log(0.01), math.log(1.5))), 0.01, 1.5)
    return {"populations": populations, "solid": solid, "panel_cell": panel_cell, "panel_owner": panel_owner, "panel_count": panel_count, "panel_area": panel_area, "observers": observers, "frequencies": frequencies}


VELOCITIES = np.array([[0, 0, 0], [1, 0, 0], [-1, 0, 0], [0, 1, 0], [0, -1, 0], [0, 0, 1], [0, 0, -1], [1, 1, 0], [-1, -1, 0], [1, -1, 0], [-1, 1, 0], [1, 0, 1], [-1, 0, -1], [1, 0, -1], [-1, 0, 1], [0, 1, 1], [0, -1, -1], [0, 1, -1], [0, -1, 1]])
OPPOSITE = [0, 2, 1, 4, 3, 6, 5, 8, 7, 10, 9, 12, 11, 14, 13, 16, 15, 18, 17]
LATTICE_WEIGHTS = [1.0 / 3.0] + [1.0 / 18.0] * 6 + [1.0 / 36.0] * 12
base_density = 19.0
sound_factor = math.sqrt(3.0)

def relaxation():
    along_x = VELOCITIES[:, 0]
    along_y = VELOCITIES[:, 1]
    along_z = VELOCITIES[:, 2]
    constant = np.ones(19)
    raw_list = [constant, along_x, along_y, along_z, along_x * along_x, along_y * along_y, along_z * along_z, along_x * along_y, along_x * along_z, along_y * along_z, along_x * along_x * along_y, along_x * along_x * along_z, along_y * along_y * along_x, along_y * along_y * along_z, along_z * along_z * along_x, along_z * along_z * along_y, along_x * along_x * along_y * along_y, along_x * along_x * along_z * along_z, along_y * along_y * along_z * along_z]
    basis = []
    for vector in raw_list:
        column = np.array(vector) * 1.0
        for previous in basis:
            column = column - previous * (column @ previous) / (previous @ previous)
        basis.append(column)
    matrix = np.stack(basis)
    rate_list = np.array([0.0] * 4 + [1.8] * 6 + [1.4] * 6 + [1.2] * 3)
    inverse = matrix.T / np.sum(matrix * matrix, axis=1)[None, :]
    return inverse @ (rate_list[:, None] * matrix)

def collide(current, solid_mask):
    velocity_table = jnp.asarray(VELOCITIES, jnp.float32)
    weight_table = jnp.asarray(np.array(LATTICE_WEIGHTS), jnp.float32)
    relax_matrix = jnp.asarray(relaxation(), jnp.float32)
    density = lax.optimization_barrier(jnp.sum(current, axis=0))
    momentum = jnp.einsum('qd,qxyz->dxyz', velocity_table, current, precision=lax.Precision.HIGHEST)
    velocity = momentum / density[None]
    projected = jnp.einsum('qd,dxyz->qxyz', velocity_table, velocity, precision=lax.Precision.HIGHEST)
    square = lax.optimization_barrier(jnp.sum(velocity * velocity, axis=0))
    equilibrium = weight_table[:, None, None, None] * density[None] * (1.0 + 3.0 * projected + 4.5 * projected * projected - 1.5 * square[None])
    relaxed = current - jnp.einsum('pq,qxyz->pxyz', relax_matrix, current - equilibrium, precision=lax.Precision.HIGHEST)
    reversed_pops = jnp.stack([current[direction] for direction in OPPOSITE])
    relaxed = jnp.where(solid_mask[None] > 0, reversed_pops, relaxed)
    return (relaxed, density, velocity)

def propagate(relaxed):
    moved = []
    for direction in range(19):
        step_x, step_y, step_z = (int(value) for value in VELOCITIES[direction])
        moved.append(jnp.roll(relaxed[direction], (step_x, step_y, step_z), axis=(0, 1, 2)))
    return jnp.stack(moved)

def panel_terms(sampled_density, sampled_velocity, panel_area, live_mask):
    normal_flux = lax.optimization_barrier(jnp.sum(sampled_velocity * panel_area, axis=0))
    thickness = sampled_density * normal_flux
    loading = (sampled_density - base_density)[None] / 3.0 * panel_area + sampled_density[None] * sampled_velocity * normal_flux[None]
    return jnp.concatenate([thickness[None], loading], axis=0) * live_mask[None]

def window_spectra(series, omega_list):
    step_total = series.shape[0]
    real_part = jnp.zeros((series.shape[1], omega_list.shape[0], series.shape[2]), jnp.float32)
    imag_part = jnp.zeros((series.shape[1], omega_list.shape[0], series.shape[2]), jnp.float32)
    for step_index in range(step_total):
        taper_weight = 0.5 - 0.5 * math.cos(2.0 * math.pi * (step_index + 0.5) / step_total)
        phase_step = omega_list * float(step_index)
        real_part = real_part + (taper_weight * jnp.cos(phase_step))[None, :, None] * series[step_index][:, None, :]
        imag_part = imag_part - (taper_weight * jnp.sin(phase_step))[None, :, None] * series[step_index][:, None, :]
    return (real_part, imag_part)

def green_sum(real_part, imag_part, coords, observers, omega_list):
    offset_x = observers[0][:, None] - coords[0][None, :]
    offset_y = observers[1][:, None] - coords[1][None, :]
    offset_z = observers[2][:, None] - coords[2][None, :]
    distance = jnp.sqrt(offset_x * offset_x + offset_y * offset_y + offset_z * offset_z)
    inverse = 1.0 / distance

    def per_freq(packed):
        omega_now, spec_re, spec_im = packed
        wave_number = omega_now * sound_factor
        radial_re = (offset_x * spec_re[1][None] + offset_y * spec_re[2][None] + offset_z * spec_re[3][None]) * inverse
        radial_im = (offset_x * spec_im[1][None] + offset_y * spec_im[2][None] + offset_z * spec_im[3][None]) * inverse
        amp_re = -omega_now * spec_im[0][None] + radial_re * inverse - wave_number * radial_im
        amp_im = omega_now * spec_re[0][None] + wave_number * radial_re + radial_im * inverse
        phase_angle = wave_number * distance
        cosine_part = jnp.cos(phase_angle)
        sine_part = jnp.sin(phase_angle)
        out_re = lax.optimization_barrier(jnp.sum(inverse * (cosine_part * amp_re + sine_part * amp_im), axis=1))
        out_im = lax.optimization_barrier(jnp.sum(inverse * (cosine_part * amp_im - sine_part * amp_re), axis=1))
        return jnp.stack([out_re, out_im])
    result = lax.map(per_freq, (omega_list, jnp.moveaxis(real_part, 1, 0), jnp.moveaxis(imag_part, 1, 0)))
    return jnp.moveaxis(result, 0, 1)

def reference(populations, solid, panel_cell, panel_owner, panel_count, panel_area, observers, frequencies):
    slot_index = jnp.arange(DEVICES * LIST, dtype=jnp.int32)
    brick_index = slot_index // LIST
    brick_x = brick_index // N_GY
    brick_y = brick_index % N_GY
    local_x = panel_cell // (CY * CZ)
    local_y = panel_cell // CZ % CY
    local_z = panel_cell % CZ
    global_x = brick_x * CX + local_x
    global_y = brick_y * CY + local_y
    coords = jnp.stack([global_x, global_y, local_z]).astype(jnp.float32)
    live_mask = (slot_index % LIST < panel_count[brick_index]).astype(jnp.float32)
    current = populations
    series = []
    for step_index in range(STEPS):
        relaxed, density, velocity = collide(current, solid)
        sampled_density = density[global_x, global_y, local_z]
        sampled_velocity = velocity[:, global_x, global_y, local_z]
        series.append(panel_terms(sampled_density, sampled_velocity, panel_area, live_mask))
        current = propagate(relaxed)
    real_part, imag_part = window_spectra(jnp.stack(series), frequencies)
    grouped = jnp.argsort(panel_owner, stable=True).astype(jnp.int32).reshape(PATCHES, DEVICES * OWN_CAP)

    def per_patch(columns):
        return green_sum(jnp.take(real_part, columns, axis=2), jnp.take(imag_part, columns, axis=2), jnp.take(coords, columns, axis=1), observers, frequencies)
    patch_spectra = lax.map(per_patch, grouped)
    return (current, patch_spectra)
```

```python
import functools
import math

import jax
import jax.numpy as jnp
import numpy as np
from jax import lax
from jax.experimental import pallas as pl
from jax.experimental.pallas import tpu as pltpu
from jax.sharding import PartitionSpec as P

F32 = jnp.float32
BF16 = jnp.bfloat16

VEL = [
    (0, 0, 0), (1, 0, 0), (-1, 0, 0), (0, 1, 0), (0, -1, 0), (0, 0, 1), (0, 0, -1),
    (1, 1, 0), (-1, -1, 0), (1, -1, 0), (-1, 1, 0), (1, 0, 1), (-1, 0, -1),
    (1, 0, -1), (-1, 0, 1), (0, 1, 1), (0, -1, -1), (0, 1, -1), (0, -1, 1),
]
NQ = 19
BX, BY, BZ = 4, 32, 128
SOLID = 19
HX = 3
Y0 = 12
YR = 56
SLOTS = 256
PATCH = 16
CAP = 16
NB = 128
NV = 16
BASE = 19.0
VMEM_LIMIT = 60 * 1024 * 1024


def x_entries(side):
    out = []
    for dist in (1, 2, 3):
        for pop in range(NQ):
            along = VEL[pop][0] * side
            if dist == 1 or (dist == 2 and along >= 0) or (dist == 3 and along > 0):
                out.append((pop, dist))
        if dist < 3:
            out.append((SOLID, dist))
    return out


X_UP = x_entries(1)
X_DOWN = x_entries(-1)
NXE = len(X_UP)


def y_entries(side):
    out, at = [], 0
    for x in range(-HX, BX + HX):
        far = -x if x < 0 else (x - BX + 1 if x >= BX else 0)
        inward = 1 if x < 0 else -1
        for pop in range(NQ + 1):
            if pop == SOLID:
                if far > 2:
                    continue
                rows = 3
            else:
                along = VEL[pop][0] * inward
                if (far == 2 and along < 0) or (far == 3 and along <= 0):
                    continue
                rows = 3 + VEL[pop][1] * side
            out.append((pop, x, rows, at))
            at += rows
    return out, at


Y_UP, NYE = y_entries(1)
Y_DOWN, NYE_DOWN = y_entries(-1)
assert NYE == NYE_DOWN


def collide(f, solid):
    pair = [f[i] + f[i + 1] for i in range(1, NQ, 2)]
    diff = [f[i] - f[i + 1] for i in range(1, NQ, 2)]
    px, py, pz, pa, pb, pc, pd, pe, pf = pair
    dx, dy, dz, da, db, dc, dd, de, df = diff
    sxy, sxz, syz = pa + pb, pc + pd, pe + pf
    qxy, qxz, qyz = pa - pb, pc - pd, pe - pf
    rho = (f[0] + px) + (py + pz) + (sxy + (sxz + syz))
    jx = dx + (da + db) + (dc + dd)
    jy = dy + (da - db) + (de + df)
    jz = dz + (dc - dd) + (de - df)
    inv = 1.0 / rho
    ux, uy, uz = jx * inv, jy * inv, jz * inv
    exx, eyy, ezz = jx * ux, jy * uy, jz * uz
    exy, exz, eyz = jx * uy, jx * uz, jy * uz
    base = rho - 1.5 * (exx + eyy + ezz)
    third = rho * (1.0 / 3.0)
    bx = (px + sxy + sxz) - third - exx
    by = (py + sxy + syz) - third - eyy
    bz = (pz + sxz + syz) - third - ezz
    trace = bx + by + bz
    out = [None] * NQ
    out[0] = -0.2 * f[0] + 0.4 * base + trace * (1.0 / 7.0)
    axis_common = base * (0.6 / 9.0) + trace * (0.6 / 7.0)
    diag_common = base * (0.6 / 18.0) + trace * (0.2 / 7.0)
    ax = [0.3 * e - 0.1 * b for e, b in ((exx, bx), (eyy, by), (ezz, bz))]
    dg = [0.15 * e - 0.1 * b for e, b in ((exx, bx), (eyy, by), (ezz, bz))]
    half = [axis_common + a - 0.1 * p for a, p in zip(ax, (px, py, pz))]
    for (i, k), e, q, (p1, p2) in (
        ((0, 1), exy, qxy, (pa, pb)),
        ((0, 2), exz, qxz, (pc, pd)),
        ((1, 2), eyz, qyz, (pe, pf)),
    ):
        common = diag_common + (dg[i] + dg[k])
        twist = 0.3 * e - 0.15 * (q - e)
        half.append(common + twist - 0.1 * p1)
        half.append(common - twist - 0.1 * p2)
    a, b = 0.7 / 3.0, 0.7 / 6.0
    flow = [jx * a, jy * a, jz * a]
    kx, ky, kz = jx * b, jy * b, jz * b
    flow += [kx + ky, kx - ky, kx + kz, kx - kz, ky + kz, ky - kz]
    for n in range(9):
        odd = flow[n] - 0.2 * diff[n]
        out[2 * n + 1] = half[n] + odd
        out[2 * n + 2] = half[n] - odd
    opposite = [0] + [i + 1 if i % 2 else i - 1 for i in range(1, NQ)]
    out = [jnp.where(solid, f[opposite[i]], out[i]) for i in range(NQ)]
    return out, rho, jx, jy, jz


def split3(v):
    hi = v.astype(BF16)
    rest = v - hi.astype(F32)
    mid = rest.astype(BF16)
    lo = (rest - mid.astype(F32)).astype(BF16)
    return hi, mid, lo


def dot(a, b):
    return jnp.dot(a, b, preferred_element_type=F32)


def sample(moments, table, column, rows):
    row_hot = (
        lax.broadcasted_iota(jnp.int32, (SLOTS, rows), 1).astype(F32) == table[:, column : column + 1]
    ).astype(F32).astype(BF16)
    lane = lax.broadcasted_iota(jnp.int32, (SLOTS, BZ), 1).astype(F32)
    z_hot = lane == table[:, 2:3]
    columns = []
    for q in range(4):
        hi, mid, lo = split3(moments[q])
        got = dot(row_hot, hi) + dot(row_hot, mid) + dot(row_hot, lo)
        columns.append(jnp.sum(jnp.where(z_hot, got, 0.0), axis=1, keepdims=True))
    return columns


def put_message(values, out_ref):
    for part in range(2):
        total = jnp.zeros((PATCH, 128), F32)
        for r in range(8):
            at = (part * 8 + r) * PATCH
            block = values[at : at + PATCH, :]
            total = total + (pltpu.roll(block, r * NV, axis=1) if r else block)
        for p in range(PATCH):
            out_ref[p * 8 : p * 8 + 8, part * 128 : part * 128 + 128] = jnp.broadcast_to(
                total[p : p + 1, :], (8, 128)
            )


def lanes_of(columns, start=0):
    lane = lax.broadcasted_iota(jnp.int32, (SLOTS, 128), 1)
    out = jnp.zeros((SLOTS, 128), F32)
    for i, column in enumerate(columns):
        out = jnp.where(lane == start + i, column, out)
    return out


def first_kernel(
    count_ref, f_ref, solid_ref, cell_ref, owner_ref, area_ref,
    relaxed_ref, up_ref, down_ref, table_ref, message_ref, moments,
):
    @pl.loop(0, BX)
    def _(x):
        for t in range(BY // 8):
            rows = pl.ds(t * 8, 8)
            f = [f_ref[i, x, rows, :] for i in range(NQ)]
            out, rho, jx, jy, jz = collide(f, solid_ref[x, rows, :] > 0)
            for i in range(NQ):
                relaxed_ref[i, x, rows, :] = out[i]
            at = pl.ds(pl.multiple_of(x * BY + t * 8, 8), 8)
            for q, v in enumerate((rho, jx, jy, jz)):
                moments[q, at, :] = v

    for n, (pop, dist) in enumerate(X_UP):
        x = BX - dist
        up_ref[n] = solid_ref[x].astype(F32) if pop == SOLID else relaxed_ref[pop, x]
    for n, (pop, dist) in enumerate(X_DOWN):
        x = dist - 1
        down_ref[n] = solid_ref[x].astype(F32) if pop == SOLID else relaxed_ref[pop, x]

    cell = cell_ref[...]
    owner = owner_ref[...].astype(F32)
    local_x = cell // (BY * BZ)
    local_y = (cell // BZ) % BY
    local_z = cell % BZ
    slot = lax.broadcasted_iota(jnp.int32, (1, SLOTS), 1)
    live = (slot < count_ref[0]).astype(F32)
    gx = (lax.axis_index("gx") * BX).astype(jnp.int32)
    gy = (lax.axis_index("gy") * BY).astype(jnp.int32)
    across = jnp.broadcast_to(owner, (SLOTS, SLOTS))
    same = across.T == across
    earlier = lax.broadcasted_iota(jnp.int32, (SLOTS, SLOTS), 0) < lax.broadcasted_iota(
        jnp.int32, (SLOTS, SLOTS), 1
    )
    rank = jnp.sum(jnp.where(same & earlier, 1.0, 0.0), axis=0, keepdims=True)
    place = rank * PATCH + owner
    order = (
        lax.broadcasted_iota(jnp.int32, (SLOTS, SLOTS), 0).astype(F32)
        == jnp.broadcast_to(place, (SLOTS, SLOTS))
    ).astype(F32).astype(BF16)
    exact = [
        (local_x * BY + local_y).astype(F32),
        (local_x * (BY + 8) + local_y + 4).astype(F32),
        local_z.astype(F32),
        (local_x + gx).astype(F32),
        (local_y + gy).astype(F32),
        live,
    ]
    pad = jnp.zeros((1, SLOTS), F32)
    area = area_ref[...]
    hi, mid, lo = split3(jnp.concatenate([area, jnp.zeros((5, SLOTS), F32)], axis=0))
    first = jnp.concatenate(exact + [pad, pad], axis=0).astype(BF16)
    source = jnp.concatenate(
        [v.astype(F32) for v in (first, hi, mid, lo)] + [jnp.zeros((96, SLOTS), F32)], axis=0
    ).astype(BF16)
    raw = lax.dot_general(order, source, (((1,), (1,)), ((), ())), preferred_element_type=F32)
    area_cols = [
        raw[:, 8 + k : 9 + k] + raw[:, 16 + k : 17 + k] + raw[:, 24 + k : 25 + k] for k in range(3)
    ]
    table_ref[...] = raw
    picked = sample(moments, raw, 0, BX * BY)
    fixed = [raw[:, 3:4], raw[:, 4:5], raw[:, 2:3], raw[:, 5:6]] + area_cols
    put_message(lanes_of(fixed + picked), message_ref)


def edge_kernel(relaxed_ref, solid_ref, low_ref, high_ref, up_ref, down_ref):
    low = {(pop, -dist): n for n, (pop, dist) in enumerate(X_UP)}
    high = {(pop, BX - 1 + dist): n for n, (pop, dist) in enumerate(X_DOWN)}

    def rows_of(pop, x, start, count):
        if x < 0:
            return low_ref[low[pop, x], start : start + count, :]
        if x >= BX:
            return high_ref[high[pop, x], start : start + count, :]
        if pop == SOLID:
            return solid_ref[x, start : start + count, :].astype(F32)
        return relaxed_ref[pop, x, start : start + count, :]

    for pop, x, rows, at in Y_UP:
        up_ref[at : at + rows, :] = rows_of(pop, x, BY - rows, rows)
    for pop, x, rows, at in Y_DOWN:
        down_ref[at : at + rows, :] = rows_of(pop, x, 0, rows)


def steps_kernel(
    relaxed_ref, solid_ref, low_ref, high_ref, below_ref, above_ref, table_ref,
    out_ref, up_ref, down_ref, message_ref, ext_a, ext_b, moments,
):
    for x in range(BX):
        for pop in range(NQ):
            ext_a[pop, x + HX, Y0 : Y0 + BY, :] = relaxed_ref[pop, x]
        ext_a[SOLID, x + HX, Y0 : Y0 + BY, :] = solid_ref[x].astype(F32)
    for n, (pop, dist) in enumerate(X_UP):
        ext_a[pop, HX - dist, Y0 : Y0 + BY, :] = low_ref[n]
    for n, (pop, dist) in enumerate(X_DOWN):
        ext_a[pop, HX + BX - 1 + dist, Y0 : Y0 + BY, :] = high_ref[n]
    for pop, x, rows, at in Y_UP:
        ext_a[pop, x + HX, Y0 - rows : Y0, :] = below_ref[at : at + rows, :]
    for pop, x, rows, at in Y_DOWN:
        ext_a[pop, x + HX, Y0 + BY : Y0 + BY + rows, :] = above_ref[at : at + rows, :]

    own = lax.broadcasted_iota(jnp.int32, (8, BZ), 0)

    def step(source, target, margin, which):
        @pl.loop(HX - margin, HX + BX + margin)
        def _(x):
            for t in range(5):
                row = 8 + 8 * t
                f = []
                for i in range(NQ):
                    cx, cy, cz = VEL[i]
                    v = source[i, x - cx, pl.ds(row - cy, 8), :]
                    f.append(pltpu.roll(v, cz % BZ, axis=1) if cz else v)
                solid = ext_a[SOLID, x, pl.ds(row, 8), :] > 0.0
                out, *sums = collide(f, solid)
                if target is not None:
                    for i in range(NQ):
                        target[i, x, pl.ds(row, 8), :] = out[i]
                else:
                    for i in range(NQ):
                        out_ref[i, x - HX, pl.ds(t * 8, 8), :] = out[i]

                def keep():
                    at = pl.ds(pl.multiple_of((x - HX) * (BY + 8) + t * 8, 8), 8)
                    for q, v in enumerate(sums):
                        if t == 0:
                            v = jnp.where(own >= 4, v, 0.0)
                        if t == 4:
                            v = jnp.where(own < 4, v, 0.0)
                        moments[which, q, at, :] = v

                if margin == 0:
                    keep()
                else:
                    pl.when((x >= HX) & (x < HX + BX))(keep)

    step(ext_a, ext_b, 2, 0)
    step(ext_b, ext_a, 1, 1)
    step(ext_a, None, 0, 2)
    n = 0
    m = 0
    for pop in range(NQ):
        if VEL[pop][0] > 0:
            up_ref[n] = out_ref[pop, BX - 1]
            n += 1
        if VEL[pop][0] < 0:
            down_ref[m] = out_ref[pop, 0]
            m += 1
    table = table_ref[...]
    columns = []
    for which in range(3):
        columns += sample(moments.at[which], table, 1, BX * (BY + 8))
    put_message(lanes_of(columns), message_ref)


def last_kernel(relaxed_ref, low_ref, high_ref, out_ref):
    n = 0
    m = 0
    for pop in range(NQ):
        cx, cy, cz = VEL[pop]
        for x in range(BX):
            for t in range(BY // 8):
                row = 4 + 8 * t - cy
                if x - cx < 0:
                    v = low_ref[n, row : row + 8, :]
                elif x - cx >= BX:
                    v = high_ref[m, row : row + 8, :]
                else:
                    v = relaxed_ref[pop, x - cx, row : row + 8, :]
                out_ref[pop, x, t * 8 : t * 8 + 8, :] = (
                    pltpu.roll(v, cz % BZ, axis=1) if cz else v
                )
        n += cx > 0
        m += cx < 0


def fit(fun, degree, odd):
    count = 400
    x = 0.25 + 0.25 * np.cos(np.pi * (np.arange(count) + 0.5) / count)
    powers = np.stack([x ** (2 * k + odd) for k in range(degree)], axis=1)
    weight = np.ones(count)
    best = None
    for _ in range(200):
        coef = np.linalg.lstsq(powers * weight[:, None], fun(x) * weight, rcond=None)[0]
        error = np.abs(powers @ coef - fun(x))
        if best is None or error.max() < best[0]:
            best = (error.max(), coef)
        weight = weight * (0.5 + error / error.max()) ** 0.5
        weight = weight / weight.max()
    return [float(c) for c in best[1]]


ROOT2 = math.sqrt(2.0)
SIN_POLY = fit(lambda x: ROOT2 * np.sin(np.pi * x), 5, 1)
COS_POLY = fit(lambda x: ROOT2 * np.cos(np.pi * x), 6, 0)


def horner(coefs, y):
    v = y * coefs[-1] + coefs[-2]
    for c in coefs[-3::-1]:
        v = v * y + c
    return v


def sin_cos_turns(t):
    x = t - jnp.round(t)
    y = x * x
    s = horner(SIN_POLY, y) * x
    c = horner(COS_POLY, y)
    return 1.0 - s * s, s * c


CHUNKS = NB * CAP // 128


def sum_kernel(freq_ref, first_ref, second_ref, obs_ref, out_ref, info, series, weights, acc, obs_lanes):
    lane = lax.broadcasted_iota(jnp.int32, (NB, 256), 1)
    first = first_ref[...]
    live = jnp.sum(jnp.where(lane % NV == 3, first, 0.0), axis=1, keepdims=True)
    lower = (
        lax.broadcasted_iota(jnp.int32, (NB, NB), 0) > lax.broadcasted_iota(jnp.int32, (NB, NB), 1)
    ).astype(F32).astype(BF16)
    live_lanes = jnp.broadcast_to(live, (NB, 128)).astype(BF16)
    offset = dot(lower, live_lanes)
    total = jnp.sum(live).astype(jnp.int32)
    chunks = (total + 127) // 128
    turned = [first[:, :128].T, first[:, 128:].T, second_ref[:, :128].T, second_ref[:, 128:].T]
    parts = []
    for r in range(CAP):
        at = (r % 8) * NV
        both = jnp.concatenate(
            [turned[r // 8][at : at + NV, :], turned[2 + r // 8][at : at + NV, :]], axis=0
        )
        parts.append(jnp.concatenate(split3(both), axis=0))
    lanes = lax.broadcasted_iota(jnp.int32, (NB, 128), 1).astype(F32)

    @pl.loop(0, chunks)
    def _(c):
        base = (c * 128).astype(F32)
        packed = jnp.zeros((6 * NV, 128), F32)
        for r in range(CAP):
            hot = ((offset + (float(r) - base)) == lanes) & (live_lanes.astype(F32) > float(r))
            packed = packed + dot(parts[r], jnp.where(hot, 1.0, 0.0).astype(BF16))
        value = packed[: 2 * NV] + packed[2 * NV : 4 * NV] + packed[4 * NV :]
        info[c] = value[0:8, :]
        area = [value[4 + k : 5 + k, :] for k in range(3)]
        keep = value[3:4, :]
        rows = []
        for s in range(4):
            at = 7 if s == 0 else 2 * NV // 2 + 4 * (s - 1)
            rho = value[at : at + 1, :]
            j = [value[at + 1 + k : at + 2 + k, :] for k in range(3)]
            scale = 1.0 / jnp.where(keep > 0.0, rho, 1.0)
            u = [v * scale for v in j]
            flux = u[0] * area[0] + u[1] * area[1] + u[2] * area[2]
            pressure = (rho - BASE) * (1.0 / 3.0)
            rows.append(rho * flux * keep)
            for k in range(3):
                rows.append((pressure * area[k] + j[k] * flux) * keep)
        series[c] = jnp.concatenate(rows, axis=0)

    gy = lax.axis_index("gy") * 8
    sub = lax.broadcasted_iota(jnp.int32, (8, 128), 0)
    omega = jnp.zeros((8, 128), F32)
    for k in range(8):
        omega = jnp.where(sub == k, freq_ref[gy + k], omega)
    cosines, sines = [], []
    for s in range(4):
        taper = 0.5 - 0.5 * math.cos(2.0 * math.pi * (s + 0.5) / 4)
        cosines.append(taper * jnp.cos(omega * float(s)))
        sines.append(-taper * jnp.sin(omega * float(s)))

    @pl.loop(0, chunks)
    def _(c):
        for comp in range(4):
            for part, factors in enumerate((cosines, sines)):
                v = factors[0] * series[c, comp : comp + 1, :]
                for s in range(1, 4):
                    v = v + factors[s] * series[c, 4 * s + comp : 4 * s + comp + 1, :]
                if comp == 0:
                    v = v * (1.0 / math.sqrt(3.0))
                weights[c, part * 4 + comp] = v

    observers = obs_ref[...]
    for k in range(3):
        obs_lanes[k] = jnp.broadcast_to(observers[k : k + 1, :], (128, 256)).T

    turns = [freq_ref[gy + k] * (math.sqrt(3.0) / (2.0 * math.pi)) for k in range(8)]
    over_k = [1.0 / (omega[k : k + 1, :] * math.sqrt(3.0)) for k in range(8)]
    over_k = [jnp.broadcast_to(v, (8, 128)) for v in over_k]

    @pl.loop(0, 32)
    def _(o):
        rows = pl.ds(pl.multiple_of(o * 8, 8), 8)
        place = [obs_lanes[k, rows, :] for k in range(3)]

        def body(c, carry):
            d = [place[k] - info[c, k : k + 1, :] for k in range(3)]
            square = d[0] * d[0] + d[1] * d[1] + d[2] * d[2]
            inv = lax.rsqrt(square)
            dist = square * inv
            n = [v * inv for v in d]
            out = []
            for k in range(8):
                cos, sin = sin_cos_turns(dist * turns[k])
                w = [weights[c, m, k : k + 1, :] for m in range(8)]
                re = n[0] * w[1] + n[1] * w[2] + n[2] * w[3]
                im = n[0] * w[5] + n[1] * w[6] + n[2] * w[7]
                near = inv * over_k[k]
                dr = near * re - (im + w[4])
                di = near * im + (re + w[0])
                cos = cos * inv
                sin = sin * inv
                out.append(carry[2 * k] + (cos * dr + sin * di))
                out.append(carry[2 * k + 1] + (cos * di - sin * dr))
            return tuple(out)

        sums = lax.fori_loop(0, chunks, body, tuple(jnp.zeros((8, 128), F32) for _ in range(16)))
        for k in range(8):
            acc[k, rows, :] = sums[2 * k]
            acc[8 + k, rows, :] = sums[2 * k + 1]

    ones = jnp.ones((8, 128), BF16)
    for k in range(16):
        whole = jnp.zeros((8, 256), F32)
        for piece in split3(acc[k]):
            whole = whole + lax.dot_general(
                ones, piece, (((1,), (1,)), ((), ())), preferred_element_type=F32
            )
        wave = freq_ref[gy + k % 8] * math.sqrt(3.0)
        out_ref[k // 8, k % 8 : k % 8 + 1, :] = whole[0:1, :] * wave


def call(kernel, shapes, scratch=(), smem=0, inputs=0, name=None, cost=1000):
    return pl.pallas_call(
        kernel,
        out_shape=[jax.ShapeDtypeStruct(s, F32) for s in shapes],
        in_specs=[pl.BlockSpec(memory_space=pltpu.SMEM)] * smem
        + [pl.BlockSpec(memory_space=pltpu.VMEM)] * (inputs - smem),
        out_specs=[pl.BlockSpec(memory_space=pltpu.VMEM)] * len(shapes),
        scratch_shapes=list(scratch),
        compiler_params=pltpu.CompilerParams(vmem_limit_bytes=VMEM_LIMIT),
        cost_estimate=pl.CostEstimate(flops=cost, bytes_accessed=cost, transcendentals=0),
        name=name,
    )


def ring(axis, up, down):
    count = lax.axis_size(axis)
    forward = [(i, (i + 1) % count) for i in range(count)]
    backward = [((i + 1) % count, i) for i in range(count)]
    return lax.ppermute(up, axis, forward), lax.ppermute(down, axis, backward)


def exchange(message):
    return lax.all_to_all(message, ("gx", "gy"), split_axis=0, concat_axis=0, tiled=True)


def local(
    populations, solid, panel_cell, panel_owner, panel_count, panel_area, observers, frequencies
):
    cell = panel_cell.reshape(1, SLOTS)
    owner = panel_owner.reshape(1, SLOTS)
    relaxed, up, down, table, message_a = call(
        first_kernel,
        [(NQ, BX, BY, BZ), (NXE, BY, BZ), (NXE, BY, BZ), (SLOTS, 128), (NB, 256)],
        [pltpu.VMEM((4, BX * BY, BZ), F32)],
        smem=1,
        inputs=6,
        name="first",
    )(panel_count, populations, solid, cell, owner, panel_area)
    low, high = ring("gx", up, down)
    y_up, y_down = call(edge_kernel, [(NYE, BZ)] * 2, inputs=4, name="edge")(
        relaxed, solid, low, high
    )
    below, above = ring("gy", y_up, y_down)
    got_a = exchange(message_a)
    relaxed, up, down, message_b = call(
        steps_kernel,
        [(NQ, BX, BY + 8, BZ), (5, BY + 8, BZ), (5, BY + 8, BZ), (NB, 256)],
        [
            pltpu.VMEM((NQ + 1, BX + 2 * HX, YR, BZ), F32),
            pltpu.VMEM((NQ, BX + 2 * HX, YR, BZ), F32),
            pltpu.VMEM((3, 4, BX * (BY + 8), BZ), F32),
        ],
        inputs=7,
        name="steps",
    )(relaxed, solid, low, high, below, above, table)
    got_b = exchange(message_b)
    low, high = ring("gx", up, down)
    (current,) = call(last_kernel, [(NQ, BX, BY, BZ)], inputs=3, name="last")(relaxed, low, high)
    (spectra,) = call(
        sum_kernel,
        [(2, 8, 256)],
        [
            pltpu.VMEM((CHUNKS, 8, 128), F32),
            pltpu.VMEM((CHUNKS, 16, 128), F32),
            pltpu.VMEM((CHUNKS, 8, 8, 128), F32),
            pltpu.VMEM((16, 256, 128), F32),
            pltpu.VMEM((3, 256, 128), F32),
        ],
        smem=1,
        inputs=4,
        name="sums",
    )(frequencies, got_a, got_b, observers)
    return current, spectra[None]


def solution(mesh):
    return jax.shard_map(
        local,
        mesh=mesh,
        in_specs=(
            P(None, "gx", "gy", None),
            P("gx", "gy", None),
            P(("gx", "gy")),
            P(("gx", "gy")),
            P(("gx", "gy")),
            P(None, ("gx", "gy")),
            P(),
            P(),
        ),
        out_specs=(P(None, "gx", "gy", None), P("gx", None, "gy", None)),
        check_vma=False,
    )
```

```python
import math

import jax
import jax.numpy as jnp
import numpy as np
from jax import lax
from jax.experimental import pallas as pl
from jax.experimental.pallas import tpu as pltpu
from jax.sharding import PartitionSpec as P


F32 = jnp.float32
BF16 = jnp.bfloat16

VEL = [
    (0, 0, 0), (1, 0, 0), (-1, 0, 0), (0, 1, 0), (0, -1, 0), (0, 0, 1), (0, 0, -1),
    (1, 1, 0), (-1, -1, 0), (1, -1, 0), (-1, 1, 0), (1, 0, 1), (-1, 0, -1),
    (1, 0, -1), (-1, 0, 1), (0, 1, 1), (0, -1, -1), (0, 1, -1), (0, -1, 1),
]
NQ = 19
BX, BY, BZ = 4, 32, 128
SOLID = 19
HX = 3
Y0 = 12
YR = 56
SLOTS = 256
PATCH = 16
CAP = 16
NB = 128
NV = 16
BASE = 19.0


def x_entries(side):
    out = []
    for dist in (1, 2, 3):
        for pop in range(NQ):
            along = VEL[pop][0] * side
            if dist == 1 or (dist == 2 and along >= 0) or (dist == 3 and along > 0):
                out.append((pop, dist))
        if dist < 3:
            out.append((SOLID, dist))
    return out


X_UP = x_entries(1)
X_DOWN = x_entries(-1)
NXE = len(X_UP)


def y_entries(side):
    out, at = [], 0
    for x in range(-HX, BX + HX):
        far = -x if x < 0 else (x - BX + 1 if x >= BX else 0)
        inward = 1 if x < 0 else -1
        for pop in range(NQ + 1):
            if pop == SOLID:
                if far > 2:
                    continue
                rows = 3
            else:
                along = VEL[pop][0] * inward
                if (far == 2 and along < 0) or (far == 3 and along <= 0):
                    continue
                rows = 3 + VEL[pop][1] * side
            out.append((pop, x, rows, at))
            at += rows
    return out, at


Y_UP, NYE = y_entries(1)
Y_DOWN, NYE_DOWN = y_entries(-1)
assert NYE == NYE_DOWN


def collide(f, solid):
    pair = [f[i] + f[i + 1] for i in range(1, NQ, 2)]
    diff = [f[i] - f[i + 1] for i in range(1, NQ, 2)]
    px, py, pz, pa, pb, pc, pd, pe, pf = pair
    dx, dy, dz, da, db, dc, dd, de, df = diff
    sxy, sxz, syz = pa + pb, pc + pd, pe + pf
    qxy, qxz, qyz = pa - pb, pc - pd, pe - pf
    rho = (f[0] + px) + (py + pz) + (sxy + (sxz + syz))
    jx = dx + (da + db) + (dc + dd)
    jy = dy + (da - db) + (de + df)
    jz = dz + (dc - dd) + (de - df)
    inv = 1.0 / rho
    ux, uy, uz = jx * inv, jy * inv, jz * inv
    exx, eyy, ezz = jx * ux, jy * uy, jz * uz
    exy, exz, eyz = jx * uy, jx * uz, jy * uz
    base = rho - 1.5 * (exx + eyy + ezz)
    third = rho * (1.0 / 3.0)
    bx = (px + sxy + sxz) - third - exx
    by = (py + sxy + syz) - third - eyy
    bz = (pz + sxz + syz) - third - ezz
    trace = bx + by + bz
    out = [None] * NQ
    out[0] = -0.2 * f[0] + 0.4 * base + trace * (1.0 / 7.0)
    axis_common = base * (0.6 / 9.0) + trace * (0.6 / 7.0)
    diag_common = base * (0.6 / 18.0) + trace * (0.2 / 7.0)
    ax = [0.3 * e - 0.1 * b for e, b in ((exx, bx), (eyy, by), (ezz, bz))]
    dg = [0.15 * e - 0.1 * b for e, b in ((exx, bx), (eyy, by), (ezz, bz))]
    half = [axis_common + a - 0.1 * p for a, p in zip(ax, (px, py, pz))]
    for (i, k), e, q, (p1, p2) in (
        ((0, 1), exy, qxy, (pa, pb)),
        ((0, 2), exz, qxz, (pc, pd)),
        ((1, 2), eyz, qyz, (pe, pf)),
    ):
        common = diag_common + (dg[i] + dg[k])
        twist = 0.3 * e - 0.15 * (q - e)
        half.append(common + twist - 0.1 * p1)
        half.append(common - twist - 0.1 * p2)
    a, b = 0.7 / 3.0, 0.7 / 6.0
    flow = [jx * a, jy * a, jz * a]
    kx, ky, kz = jx * b, jy * b, jz * b
    flow += [kx + ky, kx - ky, kx + kz, kx - kz, ky + kz, ky - kz]
    for n in range(9):
        odd = flow[n] - 0.2 * diff[n]
        out[2 * n + 1] = half[n] + odd
        out[2 * n + 2] = half[n] - odd
    opposite = [0] + [i + 1 if i % 2 else i - 1 for i in range(1, NQ)]
    out = [jnp.where(solid, f[opposite[i]], out[i]) for i in range(NQ)]
    return out, rho, jx, jy, jz


def split3(v):
    hi = v.astype(BF16)
    rest = v - hi.astype(F32)
    mid = rest.astype(BF16)
    lo = (rest - mid.astype(F32)).astype(BF16)
    return hi, mid, lo


def dot(a, b):
    return jnp.dot(a, b, preferred_element_type=F32)


def sample(moments, table, column, rows):
    row_hot = (
        lax.broadcasted_iota(jnp.int32, (SLOTS, rows), 1).astype(F32) == table[:, column : column + 1]
    ).astype(F32).astype(BF16)
    lane = lax.broadcasted_iota(jnp.int32, (SLOTS, BZ), 1).astype(F32)
    z_hot = lane == table[:, 2:3]
    columns = []
    for q in range(4):
        hi, mid, lo = split3(moments[q])
        got = dot(row_hot, hi) + dot(row_hot, mid) + dot(row_hot, lo)
        columns.append(jnp.sum(jnp.where(z_hot, got, 0.0), axis=1, keepdims=True))
    return columns


def put_message(values, out_ref):
    halves = []
    for part in range(2):
        total = jnp.zeros((PATCH, 128), F32)
        for r in range(8):
            at = (part * 8 + r) * PATCH
            block = values[at : at + PATCH, :]
            total = total + (pltpu.roll(block, r * NV, axis=1) if r else block)
        halves.append(total)
    odd = lax.broadcasted_iota(jnp.int32, (16, 128), 0) % 2 == 1
    for p in range(PATCH):
        out_ref[p * 16 : p * 16 + 16, :] = jnp.where(
            odd,
            jnp.broadcast_to(halves[1][p : p + 1, :], (16, 128)),
            jnp.broadcast_to(halves[0][p : p + 1, :], (16, 128)),
        )


def lanes_of(columns, start=0):
    lane = lax.broadcasted_iota(jnp.int32, (SLOTS, 128), 1)
    out = jnp.zeros((SLOTS, 128), F32)
    for i, column in enumerate(columns):
        out = jnp.where(lane == start + i, column, out)
    return out


def turn(v, pop):
    step = VEL[pop][2]
    return pltpu.roll(v, step % BZ, axis=1) if step else v


def first_kernel(f_ref, solid_ref, relaxed_ref, up_ref, down_ref, moments_ref):
    @pl.loop(0, BX)
    def _(x):
        for t in range(BY // 8):
            rows = pl.ds(t * 8, 8)
            f = [f_ref[i, x, rows, :] for i in range(NQ)]
            out, *sums = collide(f, solid_ref[x, rows, :] > 0)
            for i in range(NQ):
                relaxed_ref[i, x, rows, :] = turn(out[i], i)
            at = pl.ds(pl.multiple_of(x * BY + t * 8, 8), 8)
            for q, v in enumerate(sums):
                moments_ref[q, at, :] = v

    for n, (pop, dist) in enumerate(X_UP):
        x = BX - dist
        up_ref[n] = solid_ref[x].astype(F32) if pop == SOLID else relaxed_ref[pop, x]
    for n, (pop, dist) in enumerate(X_DOWN):
        x = dist - 1
        down_ref[n] = solid_ref[x].astype(F32) if pop == SOLID else relaxed_ref[pop, x]


def slots_kernel(count_ref, cell_ref, owner_ref, area_ref, moments_ref, table_ref, message_ref):
    cell = cell_ref[...]
    owner = owner_ref[...].astype(F32)
    local_x = cell // (BY * BZ)
    local_y = (cell // BZ) % BY
    local_z = cell % BZ
    slot = lax.broadcasted_iota(jnp.int32, (1, SLOTS), 1)
    live = (slot < count_ref[0]).astype(F32)
    gx = (lax.axis_index("gx") * BX).astype(jnp.int32)
    gy = (lax.axis_index("gy") * BY).astype(jnp.int32)
    across = jnp.broadcast_to(owner, (SLOTS, SLOTS))
    same = across.T == across
    earlier = lax.broadcasted_iota(jnp.int32, (SLOTS, SLOTS), 0) < lax.broadcasted_iota(
        jnp.int32, (SLOTS, SLOTS), 1
    )
    rank = jnp.sum(jnp.where(same & earlier, 1.0, 0.0), axis=0, keepdims=True)
    place = rank * PATCH + owner
    order = (
        lax.broadcasted_iota(jnp.int32, (SLOTS, SLOTS), 0).astype(F32)
        == jnp.broadcast_to(place, (SLOTS, SLOTS))
    ).astype(F32).astype(BF16)
    exact = [
        (local_x * BY + local_y).astype(F32),
        (local_x * (BY + 8) + local_y + 4).astype(F32),
        local_z.astype(F32),
        (local_x + gx).astype(F32),
        (local_y + gy).astype(F32),
        live,
    ]
    pad = jnp.zeros((1, SLOTS), F32)
    area = area_ref[...]
    hi, mid, lo = split3(jnp.concatenate([area, jnp.zeros((5, SLOTS), F32)], axis=0))
    first = jnp.concatenate(exact + [pad, pad], axis=0).astype(BF16)
    source = jnp.concatenate(
        [v.astype(F32) for v in (first, hi, mid, lo)] + [jnp.zeros((96, SLOTS), F32)], axis=0
    ).astype(BF16)
    raw = lax.dot_general(order, source, (((1,), (1,)), ((), ())), preferred_element_type=F32)
    area_cols = [
        raw[:, 8 + k : 9 + k] + raw[:, 16 + k : 17 + k] + raw[:, 24 + k : 25 + k] for k in range(3)
    ]
    table_ref[...] = raw
    picked = sample([moments_ref[q] for q in range(4)], raw, 0, BX * BY)
    fixed = [raw[:, 3:4], raw[:, 4:5], raw[:, 2:3], raw[:, 5:6]] + area_cols
    put_message(lanes_of(fixed + picked), message_ref)


def edge_kernel(relaxed_ref, solid_ref, low_ref, high_ref, up_ref, down_ref):
    low = {(pop, -dist): n for n, (pop, dist) in enumerate(X_UP)}
    high = {(pop, BX - 1 + dist): n for n, (pop, dist) in enumerate(X_DOWN)}

    def rows_of(pop, x, start, count):
        if x < 0:
            return low_ref[low[pop, x], start : start + count, :]
        if x >= BX:
            return high_ref[high[pop, x], start : start + count, :]
        if pop == SOLID:
            return solid_ref[x, start : start + count, :].astype(F32)
        return relaxed_ref[pop, x, start : start + count, :]

    for pop, x, rows, at in Y_UP:
        up_ref[at : at + rows, :] = rows_of(pop, x, BY - rows, rows)
    for pop, x, rows, at in Y_DOWN:
        down_ref[at : at + rows, :] = rows_of(pop, x, 0, rows)


def steps_kernel(
    relaxed_ref, solid_ref, low_ref, high_ref, below_ref, above_ref, table_ref,
    out_ref, up_ref, down_ref, message_ref, ext_a, ext_b, moments,
):
    for x in range(BX):
        for pop in range(NQ):
            ext_a[pop, x + HX, Y0 : Y0 + BY, :] = relaxed_ref[pop, x]
        ext_a[SOLID, x + HX, Y0 : Y0 + BY, :] = solid_ref[x].astype(F32)
    for n, (pop, dist) in enumerate(X_UP):
        ext_a[pop, HX - dist, Y0 : Y0 + BY, :] = low_ref[n]
    for n, (pop, dist) in enumerate(X_DOWN):
        ext_a[pop, HX + BX - 1 + dist, Y0 : Y0 + BY, :] = high_ref[n]
    for pop, x, rows, at in Y_UP:
        ext_a[pop, x + HX, Y0 - rows : Y0, :] = below_ref[at : at + rows, :]
    for pop, x, rows, at in Y_DOWN:
        ext_a[pop, x + HX, Y0 + BY : Y0 + BY + rows, :] = above_ref[at : at + rows, :]

    own = lax.broadcasted_iota(jnp.int32, (8, BZ), 0)

    def step(source, target, margin, which):
        @pl.loop(HX - margin, HX + BX + margin)
        def _(x):
            for t in range(5):
                row = 8 + 8 * t
                f = []
                for i in range(NQ):
                    cx, cy, _ = VEL[i]
                    f.append(source[i, x - cx, pl.ds(row - cy, 8), :])
                solid = ext_a[SOLID, x, pl.ds(row, 8), :] > 0.0
                out, *sums = collide(f, solid)
                if target is not None:
                    for i in range(NQ):
                        target[i, x, pl.ds(row, 8), :] = turn(out[i], i)
                else:
                    for i in range(NQ):
                        out_ref[i, x - HX, pl.ds(t * 8, 8), :] = turn(out[i], i)

                at = pl.ds(pl.multiple_of(x * (BY + 8) + t * 8, 8), 8)
                for q, v in enumerate(sums):
                    if t == 0:
                        v = jnp.where(own >= 4, v, 0.0)
                    if t == 4:
                        v = jnp.where(own < 4, v, 0.0)
                    moments[which, q, at, :] = v

    step(ext_a, ext_b, 2, 0)
    step(ext_b, ext_a, 1, 1)
    step(ext_a, None, 0, 2)
    n = 0
    m = 0
    for pop in range(NQ):
        if VEL[pop][0] > 0:
            up_ref[n] = out_ref[pop, BX - 1]
            n += 1
        if VEL[pop][0] < 0:
            down_ref[m] = out_ref[pop, 0]
            m += 1
    table = table_ref[...]
    columns = []
    for which in range(3):
        inside = pl.ds(HX * (BY + 8), BX * (BY + 8))
        sums = [moments[which, q, inside, :] for q in range(4)]
        columns += sample(sums, table, 1, BX * (BY + 8))
    put_message(lanes_of(columns), message_ref)


def last_kernel(relaxed_ref, low_ref, high_ref, out_ref):
    n = 0
    m = 0
    for pop in range(NQ):
        cx, cy, _ = VEL[pop]
        for x in range(BX):
            for t in range(BY // 8):
                row = 4 + 8 * t - cy
                if x - cx < 0:
                    v = low_ref[n, row : row + 8, :]
                elif x - cx >= BX:
                    v = high_ref[m, row : row + 8, :]
                else:
                    v = relaxed_ref[pop, x - cx, row : row + 8, :]
                out_ref[pop, x, t * 8 : t * 8 + 8, :] = v
        n += cx > 0
        m += cx < 0


def fit(fun, degree, odd):
    count = 400
    x = 0.25 + 0.25 * np.cos(np.pi * (np.arange(count) + 0.5) / count)
    powers = np.stack([x ** (2 * k + odd) for k in range(degree)], axis=1)
    weight = np.ones(count)
    best = None
    for _ in range(200):
        coef = np.linalg.lstsq(powers * weight[:, None], fun(x) * weight, rcond=None)[0]
        error = np.abs(powers @ coef - fun(x))
        if best is None or error.max() < best[0]:
            best = (error.max(), coef)
        weight = weight * (0.5 + error / error.max()) ** 0.5
        weight = weight / weight.max()
    return [float(c) for c in best[1]]


ROOT2 = math.sqrt(2.0)
SIN_POLY = fit(lambda x: ROOT2 * np.sin(np.pi * x), 5, 1)
COS_POLY = fit(lambda x: ROOT2 * np.cos(np.pi * x), 5, 0)


def horner(coefs, y):
    v = y * coefs[-1] + coefs[-2]
    for c in coefs[-3::-1]:
        v = v * y + c
    return v


def sin_cos_turns(t):
    x = t - jnp.round(t)
    y = x * x
    s = horner(SIN_POLY, y) * x
    c = horner(COS_POLY, y)
    return 1.0 - s * s, s * c


CHUNKS = NB * CAP // 128


def sum_kernel(
    freq_ref, first_ref, second_ref, obs_ref, out_ref, info, series, weights, acc, obs_lanes, places
):
    lane = lax.broadcasted_iota(jnp.int32, (2 * NB, 128), 1)
    first = first_ref[...]
    live = jnp.sum(jnp.where(lane % NV == 3, first, 0.0), axis=1, keepdims=True)
    lower = (
        lax.broadcasted_iota(jnp.int32, (2 * NB, 2 * NB), 0)
        > lax.broadcasted_iota(jnp.int32, (2 * NB, 2 * NB), 1)
    ).astype(F32).astype(BF16)
    live_lanes = jnp.broadcast_to(live, (2 * NB, 128))
    offset = dot(lower, live_lanes.astype(BF16))
    total = jnp.sum(live).astype(jnp.int32)
    chunks = (total + 127) // 128
    for r in range(8):
        places[r] = jnp.where(live_lanes > float(r), offset + float(r), -1.0)
    turned = [first.T, second_ref[...].T]
    parts = []
    for r in range(8):
        both = jnp.concatenate([v[r * NV : r * NV + NV, :] for v in turned], axis=0)
        parts.append(jnp.concatenate(split3(both), axis=0))
    lanes = lax.broadcasted_iota(jnp.int32, (2 * NB, 128), 1)

    @pl.loop(0, chunks)
    def _(c):
        here = (lanes + c * 128).astype(F32)
        packed = jnp.zeros((6 * NV, 128), F32)
        for r in range(8):
            hot = jnp.where(places[r] == here, 1.0, 0.0).astype(BF16)
            packed = packed + dot(parts[r], hot)
        value = packed[: 2 * NV] + packed[2 * NV : 4 * NV] + packed[4 * NV :]
        info[c] = value[0:8, :]
        area = [value[4 + k : 5 + k, :] for k in range(3)]
        keep = value[3:4, :]
        rows = []
        for s in range(4):
            at = 7 if s == 0 else 2 * NV // 2 + 4 * (s - 1)
            rho = value[at : at + 1, :]
            j = [value[at + 1 + k : at + 2 + k, :] for k in range(3)]
            scale = 1.0 / jnp.where(keep > 0.0, rho, 1.0)
            u = [v * scale for v in j]
            flux = u[0] * area[0] + u[1] * area[1] + u[2] * area[2]
            pressure = (rho - BASE) * (1.0 / 3.0)
            rows.append(rho * flux * keep)
            for k in range(3):
                rows.append((pressure * area[k] + j[k] * flux) * keep)
        series[c] = jnp.concatenate(rows, axis=0)

    gy = lax.axis_index("gy") * 8
    sub = lax.broadcasted_iota(jnp.int32, (8, 128), 0)
    omega = jnp.zeros((8, 128), F32)
    for k in range(8):
        omega = jnp.where(sub == k, freq_ref[gy + k], omega)
    cosines, sines = [], []
    for s in range(4):
        taper = 0.5 - 0.5 * math.cos(2.0 * math.pi * (s + 0.5) / 4)
        cosines.append(taper * jnp.cos(omega * float(s)))
        sines.append(-taper * jnp.sin(omega * float(s)))

    @pl.loop(0, chunks)
    def _(c):
        for comp in range(4):
            for part, factors in enumerate((cosines, sines)):
                v = factors[0] * series[c, comp : comp + 1, :]
                for s in range(1, 4):
                    v = v + factors[s] * series[c, 4 * s + comp : 4 * s + comp + 1, :]
                if comp == 0:
                    v = v * (1.0 / math.sqrt(3.0))
                weights[c, part * 4 + comp] = v

    observers = obs_ref[...]
    for k in range(3):
        obs_lanes[k] = jnp.broadcast_to(observers[k : k + 1, :], (128, 256)).T

    turns = [freq_ref[gy + k] * (math.sqrt(3.0) / (2.0 * math.pi)) for k in range(8)]
    over_k = [1.0 / (omega[k : k + 1, :] * math.sqrt(3.0)) for k in range(8)]
    over_k = [jnp.broadcast_to(v, (8, 128)) for v in over_k]

    @pl.loop(0, 32)
    def _(o):
        rows = pl.ds(pl.multiple_of(o * 8, 8), 8)
        place = [obs_lanes[k, rows, :] for k in range(3)]

        def body(c, carry):
            d = [place[k] - info[c, k : k + 1, :] for k in range(3)]
            square = d[0] * d[0] + d[1] * d[1] + d[2] * d[2]
            inv = lax.rsqrt(square)
            dist = square * inv
            n = [v * inv for v in d]
            out = []
            for k in range(8):
                cos, sin = sin_cos_turns(dist * turns[k])
                w = [weights[c, m, k : k + 1, :] for m in range(8)]
                re = n[0] * w[1] + n[1] * w[2] + n[2] * w[3]
                im = n[0] * w[5] + n[1] * w[6] + n[2] * w[7]
                near = inv * over_k[k]
                dr = near * re - (im + w[4])
                di = near * im + (re + w[0])
                cos = cos * inv
                sin = sin * inv
                out.append(carry[2 * k] + (cos * dr + sin * di))
                out.append(carry[2 * k + 1] + (cos * di - sin * dr))
            return tuple(out)

        sums = lax.fori_loop(0, chunks, body, tuple(jnp.zeros((8, 128), F32) for _ in range(16)))
        for k in range(8):
            acc[k, rows, :] = sums[2 * k]
            acc[8 + k, rows, :] = sums[2 * k + 1]

    ones = jnp.ones((8, 128), BF16)
    for k in range(16):
        whole = jnp.zeros((8, 256), F32)
        for piece in split3(acc[k]):
            whole = whole + lax.dot_general(
                ones, piece, (((1,), (1,)), ((), ())), preferred_element_type=F32
            )
        wave = freq_ref[gy + k % 8] * math.sqrt(3.0)
        out_ref[k // 8, k % 8 : k % 8 + 1, :] = whole[0:1, :] * wave


def call(kernel, shapes, scratch=(), smem=0, inputs=0, cost=1000, limit=8):
    return pl.pallas_call(
        kernel,
        out_shape=[jax.ShapeDtypeStruct(s, F32) for s in shapes],
        in_specs=[pl.BlockSpec(memory_space=pltpu.SMEM)] * smem
        + [pl.BlockSpec(memory_space=pltpu.VMEM)] * (inputs - smem),
        out_specs=[pl.BlockSpec(memory_space=pltpu.VMEM)] * len(shapes),
        scratch_shapes=list(scratch),
        compiler_params=pltpu.CompilerParams(vmem_limit_bytes=limit << 20),
        cost_estimate=pl.CostEstimate(flops=cost, bytes_accessed=cost, transcendentals=0),
    )


def ring(axis, up, down):
    count = lax.axis_size(axis)
    forward = [(i, (i + 1) % count) for i in range(count)]
    backward = [((i + 1) % count, i) for i in range(count)]
    low = lax.ppermute(up, axis, forward)
    high = lax.ppermute(down, axis, backward)
    return low, high


def exchange(message):
    return lax.all_to_all(message, ("gx", "gy"), split_axis=0, concat_axis=0, tiled=True)


def run(
    populations, solid, panel_cell, panel_owner, panel_count, panel_area, observers, frequencies
):
    cell = panel_cell.reshape(1, SLOTS)
    owner = panel_owner.reshape(1, SLOTS)
    relaxed, up, down, moments = call(
        first_kernel,
        [(NQ, BX, BY, BZ), (NXE, BY, BZ), (NXE, BY, BZ), (4, BX * BY, BZ)],
        inputs=2,
        limit=12,
    )(populations, solid)
    table, message_a = call(
        slots_kernel, [(SLOTS, 128), (2 * NB, 128)], smem=1, inputs=5
    )(panel_count, cell, owner, panel_area, moments)
    low, high = ring("gx", up, down)
    y_up, y_down = call(edge_kernel, [(NYE, BZ)] * 2, inputs=4)(relaxed, solid, low, high)
    below, above = ring("gy", y_up, y_down)
    got_a = exchange(message_a)
    relaxed, up, down, message_b = call(
        steps_kernel,
        [(NQ, BX, BY + 8, BZ), (5, BY + 8, BZ), (5, BY + 8, BZ), (2 * NB, 128)],
        [
            pltpu.VMEM((NQ + 1, BX + 2 * HX, YR, BZ), F32),
            pltpu.VMEM((NQ, BX + 2 * HX, YR, BZ), F32),
            pltpu.VMEM((3, 4, (BX + 2 * HX) * (BY + 8), BZ), F32),
        ],
        inputs=7,
        limit=28,
    )(relaxed, solid, low, high, below, above, table)
    got_b = exchange(message_b)
    low, high = ring("gx", up, down)
    (current,) = call(last_kernel, [(NQ, BX, BY, BZ)], inputs=3)(relaxed, low, high)
    (spectra,) = call(
        sum_kernel,
        [(2, 8, 256)],
        [
            pltpu.VMEM((CHUNKS, 8, 128), F32),
            pltpu.VMEM((CHUNKS, 16, 128), F32),
            pltpu.VMEM((CHUNKS, 8, 8, 128), F32),
            pltpu.VMEM((16, 256, 128), F32),
            pltpu.VMEM((3, 256, 128), F32),
            pltpu.VMEM((8, 2 * NB, 128), F32),
        ],
        smem=1,
        inputs=4,
        limit=14,
    )(frequencies, got_a, got_b, observers)
    return current, spectra[None]


def solution(mesh):
    return jax.shard_map(
        run,
        mesh=mesh,
        in_specs=(
            P(None, "gx", "gy", None),
            P("gx", "gy", None),
            P(("gx", "gy")),
            P(("gx", "gy")),
            P(("gx", "gy")),
            P(None, ("gx", "gy")),
            P(),
            P(),
        ),
        out_specs=(P(None, "gx", "gy", None), P("gx", None, "gy", None)),
        check_vma=False,
    )
```

```python
import math

import jax
import jax.numpy as jnp
import numpy as np
from jax import lax
from jax.experimental import pallas as pl
from jax.experimental.pallas import tpu as pltpu
from jax.sharding import PartitionSpec as P


F32 = jnp.float32
BF16 = jnp.bfloat16

VEL = [
    (0, 0, 0), (1, 0, 0), (-1, 0, 0), (0, 1, 0), (0, -1, 0), (0, 0, 1), (0, 0, -1),
    (1, 1, 0), (-1, -1, 0), (1, -1, 0), (-1, 1, 0), (1, 0, 1), (-1, 0, -1),
    (1, 0, -1), (-1, 0, 1), (0, 1, 1), (0, -1, -1), (0, 1, -1), (0, -1, 1),
]
NQ = 19
BX, BY, BZ = 4, 32, 128
SOLID = 19
HX = 3
Y0 = 12
YR = 56
SLOTS = 256
PATCH = 16
CAP = 16
NB = 128
NV = 16
BASE = 19.0


def x_entries(side):
    out = []
    for dist in (1, 2, 3):
        for pop in range(NQ):
            along = VEL[pop][0] * side
            if dist == 1 or (dist == 2 and along >= 0) or (dist == 3 and along > 0):
                out.append((pop, dist))
        if dist < 3:
            out.append((SOLID, dist))
    return out


X_UP = x_entries(1)
X_DOWN = x_entries(-1)
NXE = len(X_UP)


def y_entries(side):
    out, at = [], 0
    for x in range(-HX, BX + HX):
        far = -x if x < 0 else (x - BX + 1 if x >= BX else 0)
        inward = 1 if x < 0 else -1
        for pop in range(NQ + 1):
            if pop == SOLID:
                if far > 2:
                    continue
                rows = 3
            else:
                along = VEL[pop][0] * inward
                if (far == 2 and along < 0) or (far == 3 and along <= 0):
                    continue
                rows = 3 + VEL[pop][1] * side
            out.append((pop, x, rows, at))
            at += rows
    return out, at


Y_UP, NYE = y_entries(1)
Y_DOWN, NYE_DOWN = y_entries(-1)
assert NYE == NYE_DOWN


def collide(f, solid):
    pair = [f[i] + f[i + 1] for i in range(1, NQ, 2)]
    diff = [f[i] - f[i + 1] for i in range(1, NQ, 2)]
    px, py, pz, pa, pb, pc, pd, pe, pf = pair
    dx, dy, dz, da, db, dc, dd, de, df = diff
    sxy, sxz, syz = pa + pb, pc + pd, pe + pf
    qxy, qxz, qyz = pa - pb, pc - pd, pe - pf
    rho = (f[0] + px) + (py + pz) + (sxy + (sxz + syz))
    jx = dx + (da + db) + (dc + dd)
    jy = dy + (da - db) + (de + df)
    jz = dz + (dc - dd) + (de - df)
    inv = 1.0 / rho
    ux, uy, uz = jx * inv, jy * inv, jz * inv
    exx, eyy, ezz = jx * ux, jy * uy, jz * uz
    exy, exz, eyz = jx * uy, jx * uz, jy * uz
    base = rho - 1.5 * (exx + eyy + ezz)
    third = rho * (1.0 / 3.0)
    bx = (px + sxy + sxz) - third - exx
    by = (py + sxy + syz) - third - eyy
    bz = (pz + sxz + syz) - third - ezz
    trace = bx + by + bz
    out = [None] * NQ
    out[0] = -0.2 * f[0] + 0.4 * base + trace * (1.0 / 7.0)
    axis_common = base * (0.6 / 9.0) + trace * (0.6 / 7.0)
    diag_common = base * (0.6 / 18.0) + trace * (0.2 / 7.0)
    ax = [0.3 * e - 0.1 * b for e, b in ((exx, bx), (eyy, by), (ezz, bz))]
    dg = [0.15 * e - 0.1 * b for e, b in ((exx, bx), (eyy, by), (ezz, bz))]
    half = [axis_common + a - 0.1 * p for a, p in zip(ax, (px, py, pz))]
    for (i, k), e, q, (p1, p2) in (
        ((0, 1), exy, qxy, (pa, pb)),
        ((0, 2), exz, qxz, (pc, pd)),
        ((1, 2), eyz, qyz, (pe, pf)),
    ):
        common = diag_common + (dg[i] + dg[k])
        twist = 0.3 * e - 0.15 * (q - e)
        half.append(common + twist - 0.1 * p1)
        half.append(common - twist - 0.1 * p2)
    a, b = 0.7 / 3.0, 0.7 / 6.0
    flow = [jx * a, jy * a, jz * a]
    kx, ky, kz = jx * b, jy * b, jz * b
    flow += [kx + ky, kx - ky, kx + kz, kx - kz, ky + kz, ky - kz]
    for n in range(9):
        odd = flow[n] - 0.2 * diff[n]
        out[2 * n + 1] = half[n] + odd
        out[2 * n + 2] = half[n] - odd
    opposite = [0] + [i + 1 if i % 2 else i - 1 for i in range(1, NQ)]
    out = [jnp.where(solid, f[opposite[i]], out[i]) for i in range(NQ)]
    return out, rho, jx, jy, jz


def split3(v):
    hi = v.astype(BF16)
    rest = v - hi.astype(F32)
    mid = rest.astype(BF16)
    lo = (rest - mid.astype(F32)).astype(BF16)
    return hi, mid, lo


def dot(a, b):
    return jnp.dot(a, b, preferred_element_type=F32)


def sample(moments, table, column, rows):
    row_hot = (
        lax.broadcasted_iota(jnp.int32, (SLOTS, rows), 1).astype(F32) == table[:, column : column + 1]
    ).astype(F32).astype(BF16)
    lane = lax.broadcasted_iota(jnp.int32, (SLOTS, BZ), 1).astype(F32)
    z_hot = lane == table[:, 2:3]
    columns = []
    for q in range(4):
        hi, mid, lo = split3(moments[q])
        got = dot(row_hot, hi) + dot(row_hot, mid) + dot(row_hot, lo)
        columns.append(jnp.sum(jnp.where(z_hot, got, 0.0), axis=1, keepdims=True))
    return columns


def put_message(values, out_ref):
    halves = []
    for part in range(2):
        total = jnp.zeros((PATCH, 128), F32)
        for r in range(8):
            at = (part * 8 + r) * PATCH
            block = values[at : at + PATCH, :]
            total = total + (pltpu.roll(block, r * NV, axis=1) if r else block)
        halves.append(total)
    odd = lax.broadcasted_iota(jnp.int32, (16, 128), 0) % 2 == 1
    for p in range(PATCH):
        out_ref[p * 16 : p * 16 + 16, :] = jnp.where(
            odd,
            jnp.broadcast_to(halves[1][p : p + 1, :], (16, 128)),
            jnp.broadcast_to(halves[0][p : p + 1, :], (16, 128)),
        )


def lanes_of(columns, start=0):
    lane = lax.broadcasted_iota(jnp.int32, (SLOTS, 128), 1)
    out = jnp.zeros((SLOTS, 128), F32)
    for i, column in enumerate(columns):
        out = jnp.where(lane == start + i, column, out)
    return out


def turn(v, pop):
    step = VEL[pop][2]
    return pltpu.roll(v, step % BZ, axis=1) if step else v


def first_kernel(f_hbm, solid_hbm, relaxed_ref, up_ref, down_ref, moments_ref, f_ref, solid_ref, sems):
    def plane(x):
        return pltpu.make_async_copy(f_hbm.at[:, x], f_ref.at[:, x], sems.at[x])

    mask = pltpu.make_async_copy(solid_hbm, solid_ref, sems.at[BX])
    mask.start()
    for x in range(BX):
        plane(x).start()
    mask.wait()

    @pl.loop(0, BX)
    def _(x):
        plane(x).wait()
        for t in range(BY // 8):
            rows = pl.ds(t * 8, 8)
            f = [f_ref[i, x, rows, :] for i in range(NQ)]
            out, *sums = collide(f, solid_ref[x, rows, :] > 0)
            for i in range(NQ):
                relaxed_ref[i, x, rows, :] = turn(out[i], i)
            at = pl.ds(pl.multiple_of(x * BY + t * 8, 8), 8)
            for q, v in enumerate(sums):
                moments_ref[q, at, :] = v

    for n, (pop, dist) in enumerate(X_UP):
        x = BX - dist
        up_ref[n] = solid_ref[x].astype(F32) if pop == SOLID else relaxed_ref[pop, x]
    for n, (pop, dist) in enumerate(X_DOWN):
        x = dist - 1
        down_ref[n] = solid_ref[x].astype(F32) if pop == SOLID else relaxed_ref[pop, x]


def slots_kernel(count_ref, cell_ref, owner_ref, area_ref, moments_ref, table_ref, message_ref):
    cell = cell_ref[...]
    owner = owner_ref[...].astype(F32)
    local_x = cell // (BY * BZ)
    local_y = (cell // BZ) % BY
    local_z = cell % BZ
    slot = lax.broadcasted_iota(jnp.int32, (1, SLOTS), 1)
    live = (slot < count_ref[0]).astype(F32)
    gx = (lax.axis_index("gx") * BX).astype(jnp.int32)
    gy = (lax.axis_index("gy") * BY).astype(jnp.int32)
    across = jnp.broadcast_to(owner, (SLOTS, SLOTS))
    same = across.T == across
    earlier = lax.broadcasted_iota(jnp.int32, (SLOTS, SLOTS), 0) < lax.broadcasted_iota(
        jnp.int32, (SLOTS, SLOTS), 1
    )
    rank = jnp.sum(jnp.where(same & earlier, 1.0, 0.0), axis=0, keepdims=True)
    place = rank * PATCH + owner
    order = (
        lax.broadcasted_iota(jnp.int32, (SLOTS, SLOTS), 0).astype(F32)
        == jnp.broadcast_to(place, (SLOTS, SLOTS))
    ).astype(F32).astype(BF16)
    exact = [
        (local_x * BY + local_y).astype(F32),
        (local_x * (BY + 8) + local_y + 4).astype(F32),
        local_z.astype(F32),
        (local_x + gx).astype(F32),
        (local_y + gy).astype(F32),
        live,
    ]
    pad = jnp.zeros((1, SLOTS), F32)
    area = area_ref[...]
    hi, mid, lo = split3(jnp.concatenate([area, jnp.zeros((5, SLOTS), F32)], axis=0))
    first = jnp.concatenate(exact + [pad, pad], axis=0).astype(BF16)
    source = jnp.concatenate(
        [v.astype(F32) for v in (first, hi, mid, lo)] + [jnp.zeros((96, SLOTS), F32)], axis=0
    ).astype(BF16)
    raw = lax.dot_general(order, source, (((1,), (1,)), ((), ())), preferred_element_type=F32)
    area_cols = [
        raw[:, 8 + k : 9 + k] + raw[:, 16 + k : 17 + k] + raw[:, 24 + k : 25 + k] for k in range(3)
    ]
    table_ref[...] = raw
    picked = sample([moments_ref[q] for q in range(4)], raw, 0, BX * BY)
    fixed = [raw[:, 3:4], raw[:, 4:5], raw[:, 2:3], raw[:, 5:6]] + area_cols
    put_message(lanes_of(fixed + picked), message_ref)


def edge_kernel(relaxed_ref, solid_ref, low_ref, high_ref, up_ref, down_ref):
    low = {(pop, -dist): n for n, (pop, dist) in enumerate(X_UP)}
    high = {(pop, BX - 1 + dist): n for n, (pop, dist) in enumerate(X_DOWN)}

    def rows_of(pop, x, start, count):
        if x < 0:
            return low_ref[low[pop, x], start : start + count, :]
        if x >= BX:
            return high_ref[high[pop, x], start : start + count, :]
        if pop == SOLID:
            return solid_ref[x, start : start + count, :].astype(F32)
        return relaxed_ref[pop, x, start : start + count, :]

    for pop, x, rows, at in Y_UP:
        up_ref[at : at + rows, :] = rows_of(pop, x, BY - rows, rows)
    for pop, x, rows, at in Y_DOWN:
        down_ref[at : at + rows, :] = rows_of(pop, x, 0, rows)


def steps_kernel(
    relaxed_ref, solid_ref, low_ref, high_ref, below_ref, above_ref, table_ref,
    out_hbm, up_ref, down_ref, message_ref, ext_a, ext_b, moments, out_ref, sem,
):
    for x in range(BX):
        for pop in range(NQ):
            ext_a[pop, x + HX, Y0 : Y0 + BY, :] = relaxed_ref[pop, x]
        ext_a[SOLID, x + HX, Y0 : Y0 + BY, :] = solid_ref[x].astype(F32)
    for n, (pop, dist) in enumerate(X_UP):
        ext_a[pop, HX - dist, Y0 : Y0 + BY, :] = low_ref[n]
    for n, (pop, dist) in enumerate(X_DOWN):
        ext_a[pop, HX + BX - 1 + dist, Y0 : Y0 + BY, :] = high_ref[n]
    for pop, x, rows, at in Y_UP:
        ext_a[pop, x + HX, Y0 - rows : Y0, :] = below_ref[at : at + rows, :]
    for pop, x, rows, at in Y_DOWN:
        ext_a[pop, x + HX, Y0 + BY : Y0 + BY + rows, :] = above_ref[at : at + rows, :]

    own = lax.broadcasted_iota(jnp.int32, (8, BZ), 0)

    def step(source, target, margin, which):
        @pl.loop(HX - margin, HX + BX + margin)
        def _(x):
            for t in range(5):
                row = 8 + 8 * t
                f = []
                for i in range(NQ):
                    cx, cy, _ = VEL[i]
                    f.append(source[i, x - cx, pl.ds(row - cy, 8), :])
                solid = ext_a[SOLID, x, pl.ds(row, 8), :] > 0.0
                out, *sums = collide(f, solid)
                for i in range(NQ):
                    target[i, x, pl.ds(row, 8), :] = turn(out[i], i)

                at = pl.ds(pl.multiple_of(x * (BY + 8) + t * 8, 8), 8)
                for q, v in enumerate(sums):
                    if t == 0:
                        v = jnp.where(own >= 4, v, 0.0)
                    if t == 4:
                        v = jnp.where(own < 4, v, 0.0)
                    moments[which, q, at, :] = v

    step(ext_a, ext_b, 2, 0)
    step(ext_b, ext_a, 1, 1)
    step(ext_a, ext_b, 0, 2)
    n = 0
    m = 0
    for pop in range(NQ):
        cx, cy, _ = VEL[pop]
        if cx > 0:
            up_ref[n] = ext_b[pop, HX + BX - 1, 8 : 48, :]
            n += 1
        if cx < 0:
            down_ref[m] = ext_b[pop, HX, 8 : 48, :]
            m += 1
        for x in range(max(cx, 0), BX + min(cx, 0)):
            out_ref[pop, x] = ext_b[pop, x + HX - cx, Y0 - cy : Y0 - cy + BY, :]
    result = pltpu.make_async_copy(out_ref, out_hbm, sem)
    result.start()
    table = table_ref[...]
    columns = []
    for which in range(3):
        inside = pl.ds(HX * (BY + 8), BX * (BY + 8))
        sums = [moments[which, q, inside, :] for q in range(4)]
        columns += sample(sums, table, 1, BX * (BY + 8))
    put_message(lanes_of(columns), message_ref)
    result.wait()


EDGES = [(pop, 0) for pop in range(NQ) if VEL[pop][0] > 0] + [
    (pop, BX - 1) for pop in range(NQ) if VEL[pop][0] < 0
]


def last_kernel(given_ref, low_ref, high_ref, out_ref, planes, sems):
    copies = []
    for n, (pop, x) in enumerate(EDGES):
        source = low_ref.at[n] if x == 0 else high_ref.at[n - 5]
        row = 4 - VEL[pop][1]
        planes[n] = source[row : row + BY, :]
        copies.append(pltpu.make_async_copy(planes.at[n], out_ref.at[pop, x], sems.at[n]))
        copies[-1].start()
    for copy in copies:
        copy.wait()


def fit(fun, degree, odd):
    count = 400
    x = 0.25 + 0.25 * np.cos(np.pi * (np.arange(count) + 0.5) / count)
    powers = np.stack([x ** (2 * k + odd) for k in range(degree)], axis=1)
    weight = np.ones(count)
    best = None
    for _ in range(200):
        coef = np.linalg.lstsq(powers * weight[:, None], fun(x) * weight, rcond=None)[0]
        error = np.abs(powers @ coef - fun(x))
        if best is None or error.max() < best[0]:
            best = (error.max(), coef)
        weight = weight * (0.5 + error / error.max()) ** 0.5
        weight = weight / weight.max()
    return [float(c) for c in best[1]]


ROOT2 = math.sqrt(2.0)
SIN_POLY = fit(lambda x: ROOT2 * np.sin(np.pi * x), 5, 1)
COS_POLY = fit(lambda x: ROOT2 * np.cos(np.pi * x), 5, 0)


def horner(coefs, y):
    v = y * coefs[-1] + coefs[-2]
    for c in coefs[-3::-1]:
        v = v * y + c
    return v


def sin_cos_turns(t):
    x = t - jnp.round(t)
    y = x * x
    s = horner(SIN_POLY, y) * x
    c = horner(COS_POLY, y)
    return 1.0 - s * s, s * c


CHUNKS = NB * CAP // 128
TILES = 2
WIDE = 4
AHEAD = 2


def parts_of(message):
    turned = message.T
    return [jnp.concatenate(split3(turned[r * NV : r * NV + NV, :]), axis=0) for r in range(8)]


def pack(parts, places, c):
    lanes = lax.broadcasted_iota(jnp.int32, (2 * NB, 128), 1)
    here = (lanes + c * 128).astype(F32)
    total = jnp.zeros((3 * NV, 128), F32)
    for r in range(8):
        hot = jnp.where(places[r] == here, 1.0, 0.0).astype(BF16)
        total = total + dot(parts[r], hot)
    return total[:NV] + total[NV : 2 * NV] + total[2 * NV :]


def distances(obs_lanes, info, c, rows):
    d = [obs_lanes[k, rows, :] - info[c, k : k + 1, :] for k in range(3)]
    square = d[0] * d[0] + d[1] * d[1] + d[2] * d[2]
    inv = lax.rsqrt(square)
    return d, inv, square * inv


def tile_rows(o, t, tiles):
    return pl.ds(pl.multiple_of(o * 8 * tiles + 8 * t, 8), 8)


def fill_places(spots, places):
    for r in range(8):
        places[r] = jnp.where(spots[1] > float(r), spots[0] + float(r), -1.0)


def count_of(total_ref):
    return (jnp.sum(total_ref[0:1, 0:1]).astype(jnp.int32) + 127) // 128


def table_kernel(
    freq_ref, first_ref, obs_ref, waves_hbm, spots, info, obs_lanes, total_ref, places, waves, sems
):
    lane = lax.broadcasted_iota(jnp.int32, (2 * NB, 128), 1)
    first = first_ref[...]
    live = jnp.sum(jnp.where(lane % NV == 3, first, 0.0), axis=1, keepdims=True)
    lower = (
        lax.broadcasted_iota(jnp.int32, (2 * NB, 2 * NB), 0)
        > lax.broadcasted_iota(jnp.int32, (2 * NB, 2 * NB), 1)
    ).astype(F32).astype(BF16)
    live_lanes = jnp.broadcast_to(live, (2 * NB, 128))
    offset = dot(lower, live_lanes.astype(BF16))
    total = jnp.sum(live)
    total_ref[...] = jnp.broadcast_to(jnp.sum(live, axis=0, keepdims=True), (8, 128))
    chunks = (total.astype(jnp.int32) + 127) // 128
    spots[0] = offset
    spots[1] = live_lanes
    fill_places(spots, places)
    parts = parts_of(first)
    observers = obs_ref[...]
    for k in range(3):
        obs_lanes[k] = jnp.broadcast_to(observers[k : k + 1, :], (128, 256)).T
    gy = lax.axis_index("gy") * 8
    turns = [freq_ref[gy + k] * (math.sqrt(3.0) / (2.0 * math.pi)) for k in range(AHEAD)]

    def store(c):
        slot = c % 2
        return pltpu.make_async_copy(waves.at[slot], waves_hbm.at[c], sems.at[slot])

    @pl.loop(0, chunks)
    def _(c):
        info[c] = pack(parts, places, c)
        slot = c % 2

        @pl.when(c >= 2)
        def _():
            store(c - 2).wait()

        @pl.loop(0, 32 // WIDE)
        def _(o):
            tiles = []
            for t in range(WIDE):
                rows = tile_rows(o, t, WIDE)
                _, inv, dist = distances(obs_lanes, info, c, rows)
                tiles.append((rows, inv, dist))
            for k in range(AHEAD):
                for rows, inv, dist in tiles:
                    cos, sin = sin_cos_turns(dist * turns[k])
                    waves[slot, 2 * k, rows, :] = cos * inv
                    waves[slot, 2 * k + 1, rows, :] = sin * inv

        store(c).start()

    @pl.when(chunks >= 2)
    def _():
        store(chunks - 2).wait()

    store(chunks - 1).wait()


def sum_kernel(
    freq_ref, waves_hbm, second_ref, spots, info, obs_lanes, total_ref, out_ref,
    series, weights, acc, places, waves, sems,
):
    chunks = count_of(total_ref)

    def load(c):
        slot = c % 2
        return pltpu.make_async_copy(waves_hbm.at[c], waves.at[slot], sems.at[slot])

    load(0).start()

    @pl.when(chunks >= 2)
    def _():
        load(1).start()

    fill_places(spots, places)
    parts = parts_of(second_ref[...])

    @pl.loop(0, chunks)
    def _(c):
        late = pack(parts, places, c)
        fixed = info[c]
        area = [fixed[4 + k : 5 + k, :] for k in range(3)]
        keep = fixed[3:4, :]
        rows = []
        for s in range(4):
            value, at = (fixed, 7) if s == 0 else (late, 4 * (s - 1))
            rho = value[at : at + 1, :]
            j = [value[at + 1 + k : at + 2 + k, :] for k in range(3)]
            scale = 1.0 / jnp.where(keep > 0.0, rho, 1.0)
            u = [v * scale for v in j]
            flux = u[0] * area[0] + u[1] * area[1] + u[2] * area[2]
            pressure = (rho - BASE) * (1.0 / 3.0)
            rows.append(rho * flux * keep)
            for k in range(3):
                rows.append((pressure * area[k] + j[k] * flux) * keep)
        series[c] = jnp.concatenate(rows, axis=0)

    gy = lax.axis_index("gy") * 8
    sub = lax.broadcasted_iota(jnp.int32, (8, 128), 0)
    omega = jnp.zeros((8, 128), F32)
    for k in range(8):
        omega = jnp.where(sub == k, freq_ref[gy + k], omega)
    cosines, sines = [], []
    for s in range(4):
        taper = 0.5 - 0.5 * math.cos(2.0 * math.pi * (s + 0.5) / 4)
        cosines.append(taper * jnp.cos(omega * float(s)))
        sines.append(-taper * jnp.sin(omega * float(s)))

    @pl.loop(0, chunks)
    def _(c):
        for comp in range(4):
            for part, factors in enumerate((cosines, sines)):
                v = factors[0] * series[c, comp : comp + 1, :]
                for s in range(1, 4):
                    v = v + factors[s] * series[c, 4 * s + comp : 4 * s + comp + 1, :]
                if comp == 0:
                    v = v * (1.0 / math.sqrt(3.0))
                weights[c, part * 4 + comp] = v

    turns = [freq_ref[gy + k] * (math.sqrt(3.0) / (2.0 * math.pi)) for k in range(8)]
    over_k = [1.0 / (omega[k : k + 1, :] * math.sqrt(3.0)) for k in range(8)]
    over_k = [jnp.broadcast_to(v, (8, 128)) for v in over_k]
    acc[...] = jnp.zeros_like(acc)

    @pl.loop(0, chunks)
    def _(c):
        slot = c % 2
        load(c).wait()

        @pl.loop(0, 32 // TILES)
        def _(o):
            tiles = []
            for t in range(TILES):
                rows = tile_rows(o, t, TILES)
                d, inv, dist = distances(obs_lanes, info, c, rows)
                tiles.append((rows, inv, dist, [v * inv for v in d]))
            for k in range(8):
                w = [weights[c, m, k : k + 1, :] for m in range(8)]
                for rows, inv, dist, n in tiles:
                    if k < AHEAD:
                        cos = waves[slot, 2 * k, rows, :]
                        sin = waves[slot, 2 * k + 1, rows, :]
                    else:
                        cos, sin = sin_cos_turns(dist * turns[k])
                        cos = cos * inv
                        sin = sin * inv
                    re = n[0] * w[1] + n[1] * w[2] + n[2] * w[3]
                    im = n[0] * w[5] + n[1] * w[6] + n[2] * w[7]
                    near = inv * over_k[k]
                    dr = near * re - (im + w[4])
                    di = near * im + (re + w[0])
                    acc[k, rows, :] += cos * dr + sin * di
                    acc[8 + k, rows, :] += cos * di - sin * dr

        @pl.when(c + 2 < chunks)
        def _():
            load(c + 2).start()

    ones = jnp.ones((8, 128), BF16)
    for k in range(16):
        whole = jnp.zeros((8, 256), F32)
        for piece in split3(acc[k]):
            whole = whole + lax.dot_general(
                ones, piece, (((1,), (1,)), ((), ())), preferred_element_type=F32
            )
        wave = freq_ref[gy + k % 8] * math.sqrt(3.0)
        out_ref[k // 8, k % 8 : k % 8 + 1, :] = whole[0:1, :] * wave


def call(
    kernel, shapes, scratch=(), smem=0, inputs=0, cost=1000, limit=8, far=0, alias=None, out_far=0
):
    near = pl.BlockSpec(memory_space=pltpu.VMEM)
    return pl.pallas_call(
        kernel,
        out_shape=[
            pltpu.HBM(s, F32) if n < out_far else jax.ShapeDtypeStruct(s, F32)
            for n, s in enumerate(shapes)
        ],
        in_specs=[pl.BlockSpec(memory_space=pltpu.SMEM)] * smem
        + [pl.BlockSpec(memory_space=pltpu.HBM)] * far
        + [near] * (inputs - smem - far),
        out_specs=[pl.BlockSpec(memory_space=pltpu.HBM)] * out_far + [near] * (len(shapes) - out_far),
        scratch_shapes=list(scratch),
        input_output_aliases=alias or {},
        compiler_params=pltpu.CompilerParams(vmem_limit_bytes=limit << 20),
        cost_estimate=pl.CostEstimate(flops=cost, bytes_accessed=cost, transcendentals=0),
    )


def far_away(array):
    return pltpu.with_memory_space_constraint(array, pltpu.HBM)


def ring(axis, up, down):
    count = lax.axis_size(axis)
    forward = [(i, (i + 1) % count) for i in range(count)]
    backward = [((i + 1) % count, i) for i in range(count)]
    low = lax.ppermute(up, axis, forward)
    high = lax.ppermute(down, axis, backward)
    return low, high


def exchange(message):
    return lax.all_to_all(message, ("gx", "gy"), split_axis=0, concat_axis=0, tiled=True)


def run(
    populations, solid, panel_cell, panel_owner, panel_count, panel_area, observers, frequencies
):
    cell = panel_cell.reshape(1, SLOTS)
    owner = panel_owner.reshape(1, SLOTS)
    relaxed, up, down, moments = call(
        first_kernel,
        [(NQ, BX, BY, BZ), (NXE, BY, BZ), (NXE, BY, BZ), (4, BX * BY, BZ)],
        [
            pltpu.VMEM((NQ, BX, BY, BZ), F32),
            pltpu.VMEM((BX, BY, BZ), jnp.int32),
            pltpu.SemaphoreType.DMA((BX + 1,)),
        ],
        inputs=2,
        far=2,
        limit=12,
    )(far_away(populations), far_away(solid))
    table, message_a = call(
        slots_kernel, [(SLOTS, 128), (2 * NB, 128)], smem=1, inputs=5
    )(panel_count, cell, owner, panel_area, moments)
    low, high = ring("gx", up, down)
    y_up, y_down = call(edge_kernel, [(NYE, BZ)] * 2, inputs=4)(relaxed, solid, low, high)
    below, above = ring("gy", y_up, y_down)
    got_a = exchange(message_a)
    current, up, down, message_b = call(
        steps_kernel,
        [(NQ, BX, BY, BZ), (5, BY + 8, BZ), (5, BY + 8, BZ), (2 * NB, 128)],
        [
            pltpu.VMEM((NQ + 1, BX + 2 * HX, YR, BZ), F32),
            pltpu.VMEM((NQ, BX + 2 * HX, YR, BZ), F32),
            pltpu.VMEM((3, 4, (BX + 2 * HX) * (BY + 8), BZ), F32),
            pltpu.VMEM((NQ, BX, BY, BZ), F32),
            pltpu.SemaphoreType.DMA,
        ],
        out_far=1,
        inputs=7,
        limit=28,
    )(relaxed, solid, low, high, below, above, table)
    got_b = exchange(message_b)
    low, high = ring("gx", up, down)
    (current,) = call(
        last_kernel,
        [(NQ, BX, BY, BZ)],
        [pltpu.VMEM((len(EDGES), BY, BZ), F32), pltpu.SemaphoreType.DMA((len(EDGES),))],
        inputs=3,
        far=1,
        out_far=1,
        alias={0: 0},
        limit=4,
    )(current, low, high)
    waves, *tables = call(
        table_kernel,
        [
            (CHUNKS, 2 * AHEAD, 256, 128),
            (2, 2 * NB, 128),
            (CHUNKS, NV, 128),
            (3, 256, 128),
            (8, 128),
        ],
        [
            pltpu.VMEM((8, 2 * NB, 128), F32),
            pltpu.VMEM((2, 2 * AHEAD, 256, 128), F32),
            pltpu.SemaphoreType.DMA((2,)),
        ],
        out_far=1,
        smem=1,
        inputs=3,
        limit=6,
    )(frequencies, got_a, observers)
    (spectra,) = call(
        sum_kernel,
        [(2, 8, 256)],
        [
            pltpu.VMEM((CHUNKS, 16, 128), F32),
            pltpu.VMEM((CHUNKS, 8, 8, 128), F32),
            pltpu.VMEM((16, 256, 128), F32),
            pltpu.VMEM((8, 2 * NB, 128), F32),
            pltpu.VMEM((2, 2 * AHEAD, 256, 128), F32),
            pltpu.SemaphoreType.DMA((2,)),
        ],
        smem=1,
        far=1,
        inputs=7,
        limit=10,
    )(frequencies, far_away(waves), got_b, *tables)
    return current, spectra[None]


def solution(mesh):
    return jax.shard_map(
        run,
        mesh=mesh,
        in_specs=(
            P(None, "gx", "gy", None),
            P("gx", "gy", None),
            P(("gx", "gy")),
            P(("gx", "gy")),
            P(("gx", "gy")),
            P(None, ("gx", "gy")),
            P(),
            P(),
        ),
        out_specs=(P(None, "gx", "gy", None), P("gx", None, "gy", None)),
        check_vma=False,
    )
```

```python
import math

import jax
import jax.numpy as jnp
import numpy as np
from jax import lax
from jax.experimental import pallas as pl
from jax.experimental.pallas import tpu as pltpu
from jax.sharding import PartitionSpec as P


F32 = jnp.float32
BF16 = jnp.bfloat16

VEL = [
    (0, 0, 0), (1, 0, 0), (-1, 0, 0), (0, 1, 0), (0, -1, 0), (0, 0, 1), (0, 0, -1),
    (1, 1, 0), (-1, -1, 0), (1, -1, 0), (-1, 1, 0), (1, 0, 1), (-1, 0, -1),
    (1, 0, -1), (-1, 0, 1), (0, 1, 1), (0, -1, -1), (0, 1, -1), (0, -1, 1),
]
NQ = 19
BX, BY, BZ = 4, 32, 128
SOLID = 19
HX = 3
Y0 = 12
YR = 56
SLOTS = 256
PATCH = 16
CAP = 16
NB = 128
NV = 16
BASE = 19.0


def x_entries(side):
    out = []
    for dist in (1, 2, 3):
        for pop in range(NQ):
            along = VEL[pop][0] * side
            if dist == 1 or (dist == 2 and along >= 0) or (dist == 3 and along > 0):
                out.append((pop, dist))
        if dist < 3:
            out.append((SOLID, dist))
    return out


X_UP = x_entries(1)
X_DOWN = x_entries(-1)
NXE = len(X_UP)


def y_entries(side):
    out, at = [], 0
    for x in range(-HX, BX + HX):
        far = -x if x < 0 else (x - BX + 1 if x >= BX else 0)
        inward = 1 if x < 0 else -1
        for pop in range(NQ + 1):
            if pop == SOLID:
                if far > 2:
                    continue
                rows = 3
            else:
                along = VEL[pop][0] * inward
                if (far == 2 and along < 0) or (far == 3 and along <= 0):
                    continue
                rows = 3 + VEL[pop][1] * side
            out.append((pop, x, rows, at))
            at += rows
    return out, at


Y_UP, NYE = y_entries(1)
Y_DOWN, NYE_DOWN = y_entries(-1)
assert NYE == NYE_DOWN


def collide(f, solid):
    pair = [f[i] + f[i + 1] for i in range(1, NQ, 2)]
    diff = [f[i] - f[i + 1] for i in range(1, NQ, 2)]
    px, py, pz, pa, pb, pc, pd, pe, pf = pair
    dx, dy, dz, da, db, dc, dd, de, df = diff
    sxy, sxz, syz = pa + pb, pc + pd, pe + pf
    qxy, qxz, qyz = pa - pb, pc - pd, pe - pf
    rho = (f[0] + px) + (py + pz) + (sxy + (sxz + syz))
    jx = dx + (da + db) + (dc + dd)
    jy = dy + (da - db) + (de + df)
    jz = dz + (dc - dd) + (de - df)
    inv = 1.0 / rho
    ux, uy, uz = jx * inv, jy * inv, jz * inv
    exx, eyy, ezz = jx * ux, jy * uy, jz * uz
    exy, exz, eyz = jx * uy, jx * uz, jy * uz
    base = rho - 1.5 * (exx + eyy + ezz)
    third = rho * (1.0 / 3.0)
    bx = (px + sxy + sxz) - third - exx
    by = (py + sxy + syz) - third - eyy
    bz = (pz + sxz + syz) - third - ezz
    trace = bx + by + bz
    out = [None] * NQ
    out[0] = -0.2 * f[0] + 0.4 * base + trace * (1.0 / 7.0)
    axis_common = base * (0.6 / 9.0) + trace * (0.6 / 7.0)
    diag_common = base * (0.6 / 18.0) + trace * (0.2 / 7.0)
    ax = [0.3 * e - 0.1 * b for e, b in ((exx, bx), (eyy, by), (ezz, bz))]
    dg = [0.15 * e - 0.1 * b for e, b in ((exx, bx), (eyy, by), (ezz, bz))]
    half = [axis_common + a - 0.1 * p for a, p in zip(ax, (px, py, pz))]
    for (i, k), e, q, (p1, p2) in (
        ((0, 1), exy, qxy, (pa, pb)),
        ((0, 2), exz, qxz, (pc, pd)),
        ((1, 2), eyz, qyz, (pe, pf)),
    ):
        common = diag_common + (dg[i] + dg[k])
        twist = 0.3 * e - 0.15 * (q - e)
        half.append(common + twist - 0.1 * p1)
        half.append(common - twist - 0.1 * p2)
    a, b = 0.7 / 3.0, 0.7 / 6.0
    flow = [jx * a, jy * a, jz * a]
    kx, ky, kz = jx * b, jy * b, jz * b
    flow += [kx + ky, kx - ky, kx + kz, kx - kz, ky + kz, ky - kz]
    for n in range(9):
        odd = flow[n] - 0.2 * diff[n]
        out[2 * n + 1] = half[n] + odd
        out[2 * n + 2] = half[n] - odd
    opposite = [0] + [i + 1 if i % 2 else i - 1 for i in range(1, NQ)]
    out = [jnp.where(solid, f[opposite[i]], out[i]) for i in range(NQ)]
    return out, rho, jx, jy, jz


def split3(v):
    hi = v.astype(BF16)
    rest = v - hi.astype(F32)
    mid = rest.astype(BF16)
    lo = (rest - mid.astype(F32)).astype(BF16)
    return hi, mid, lo


def dot(a, b):
    return jnp.dot(a, b, preferred_element_type=F32)


def sample(moments, table, column, rows):
    row_hot = (
        lax.broadcasted_iota(jnp.int32, (SLOTS, rows), 1).astype(F32) == table[:, column : column + 1]
    ).astype(F32).astype(BF16)
    row_hot = jnp.concatenate([row_hot] * 3, axis=1)
    lane = lax.broadcasted_iota(jnp.int32, (SLOTS, BZ), 1).astype(F32)
    z_hot = lane == table[:, 2:3]
    columns = []
    for q in range(4):
        got = dot(row_hot, jnp.concatenate(split3(moments[q]), axis=0))
        columns.append(jnp.sum(jnp.where(z_hot, got, 0.0), axis=1, keepdims=True))
    return columns


def put_message(values, out_ref):
    halves = []
    for part in range(2):
        total = jnp.zeros((PATCH, 128), F32)
        for r in range(8):
            at = (part * 8 + r) * PATCH
            block = values[at : at + PATCH, :]
            total = total + (pltpu.roll(block, r * NV, axis=1) if r else block)
        halves.append(total)
    odd = lax.broadcasted_iota(jnp.int32, (16, 128), 0) % 2 == 1
    for p in range(PATCH):
        out_ref[p * 16 : p * 16 + 16, :] = jnp.where(
            odd,
            jnp.broadcast_to(halves[1][p : p + 1, :], (16, 128)),
            jnp.broadcast_to(halves[0][p : p + 1, :], (16, 128)),
        )


def lanes_of(columns, start=0):
    lane = lax.broadcasted_iota(jnp.int32, (SLOTS, 128), 1)
    out = jnp.zeros((SLOTS, 128), F32)
    for i, column in enumerate(columns):
        out = jnp.where(lane == start + i, column, out)
    return out


def turn(v, pop):
    step = VEL[pop][2]
    return pltpu.roll(v, step % BZ, axis=1) if step else v


def first_kernel(f_hbm, solid_hbm, relaxed_ref, up_ref, down_ref, moments_ref, f_ref, solid_ref, sems):
    def plane(x):
        return pltpu.make_async_copy(f_hbm.at[:, x], f_ref.at[:, x], sems.at[x])

    mask = pltpu.make_async_copy(solid_hbm, solid_ref, sems.at[BX])
    mask.start()
    for x in range(BX):
        plane(x).start()
    mask.wait()

    @pl.loop(0, BX)
    def _(x):
        plane(x).wait()
        for t in range(BY // 8):
            rows = pl.ds(t * 8, 8)
            f = [f_ref[i, x, rows, :] for i in range(NQ)]
            out, *sums = collide(f, solid_ref[x, rows, :] > 0)
            for i in range(NQ):
                relaxed_ref[i, x, rows, :] = turn(out[i], i)
            at = pl.ds(pl.multiple_of(x * BY + t * 8, 8), 8)
            for q, v in enumerate(sums):
                moments_ref[q, at, :] = v

    for n, (pop, dist) in enumerate(X_UP):
        x = BX - dist
        up_ref[n] = solid_ref[x].astype(F32) if pop == SOLID else relaxed_ref[pop, x]
    for n, (pop, dist) in enumerate(X_DOWN):
        x = dist - 1
        down_ref[n] = solid_ref[x].astype(F32) if pop == SOLID else relaxed_ref[pop, x]


def slots_kernel(count_ref, cell_ref, owner_ref, area_ref, moments_ref, table_ref, message_ref):
    cell = cell_ref[...]
    owner = owner_ref[...].astype(F32)
    local_x = cell // (BY * BZ)
    local_y = (cell // BZ) % BY
    local_z = cell % BZ
    slot = lax.broadcasted_iota(jnp.int32, (1, SLOTS), 1)
    live = (slot < count_ref[0]).astype(F32)
    gx = (lax.axis_index("gx") * BX).astype(jnp.int32)
    gy = (lax.axis_index("gy") * BY).astype(jnp.int32)
    across = jnp.broadcast_to(owner, (SLOTS, SLOTS))
    same = across.T == across
    earlier = lax.broadcasted_iota(jnp.int32, (SLOTS, SLOTS), 0) < lax.broadcasted_iota(
        jnp.int32, (SLOTS, SLOTS), 1
    )
    rank = jnp.sum(jnp.where(same & earlier, 1.0, 0.0), axis=0, keepdims=True)
    place = rank * PATCH + owner
    order = (
        lax.broadcasted_iota(jnp.int32, (SLOTS, SLOTS), 0).astype(F32)
        == jnp.broadcast_to(place, (SLOTS, SLOTS))
    ).astype(F32).astype(BF16)
    exact = [
        (local_x * BY + local_y).astype(F32),
        (local_x * (BY + 8) + local_y + 4).astype(F32),
        local_z.astype(F32),
        (local_x + gx).astype(F32),
        (local_y + gy).astype(F32),
        live,
    ]
    pad = jnp.zeros((1, SLOTS), F32)
    area = area_ref[...]
    hi, mid, lo = split3(jnp.concatenate([area, jnp.zeros((5, SLOTS), F32)], axis=0))
    first = jnp.concatenate(exact + [pad, pad], axis=0).astype(BF16)
    source = jnp.concatenate(
        [v.astype(F32) for v in (first, hi, mid, lo)] + [jnp.zeros((96, SLOTS), F32)], axis=0
    ).astype(BF16)
    raw = lax.dot_general(order, source, (((1,), (1,)), ((), ())), preferred_element_type=F32)
    area_cols = [
        raw[:, 8 + k : 9 + k] + raw[:, 16 + k : 17 + k] + raw[:, 24 + k : 25 + k] for k in range(3)
    ]
    table_ref[...] = raw
    picked = sample([moments_ref[q] for q in range(4)], raw, 0, BX * BY)
    fixed = [raw[:, 3:4], raw[:, 4:5], raw[:, 2:3], raw[:, 5:6]] + area_cols
    put_message(lanes_of(fixed + picked), message_ref)


def edge_kernel(relaxed_ref, solid_ref, low_ref, high_ref, up_ref, down_ref):
    low = {(pop, -dist): n for n, (pop, dist) in enumerate(X_UP)}
    high = {(pop, BX - 1 + dist): n for n, (pop, dist) in enumerate(X_DOWN)}

    def rows_of(pop, x, start, count):
        if x < 0:
            return low_ref[low[pop, x], start : start + count, :]
        if x >= BX:
            return high_ref[high[pop, x], start : start + count, :]
        if pop == SOLID:
            return solid_ref[x, start : start + count, :].astype(F32)
        return relaxed_ref[pop, x, start : start + count, :]

    for pop, x, rows, at in Y_UP:
        up_ref[at : at + rows, :] = rows_of(pop, x, BY - rows, rows)
    for pop, x, rows, at in Y_DOWN:
        down_ref[at : at + rows, :] = rows_of(pop, x, 0, rows)


def steps_kernel(
    relaxed_ref, solid_ref, low_ref, high_ref, below_ref, above_ref, table_ref,
    out_hbm, up_ref, down_ref, message_ref, ext_a, ext_b, moments, out_ref, sem,
):
    for x in range(BX):
        for pop in range(NQ):
            ext_a[pop, x + HX, Y0 : Y0 + BY, :] = relaxed_ref[pop, x]
        ext_a[SOLID, x + HX, Y0 : Y0 + BY, :] = solid_ref[x].astype(F32)
    for n, (pop, dist) in enumerate(X_UP):
        ext_a[pop, HX - dist, Y0 : Y0 + BY, :] = low_ref[n]
    for n, (pop, dist) in enumerate(X_DOWN):
        ext_a[pop, HX + BX - 1 + dist, Y0 : Y0 + BY, :] = high_ref[n]
    for pop, x, rows, at in Y_UP:
        ext_a[pop, x + HX, Y0 - rows : Y0, :] = below_ref[at : at + rows, :]
    for pop, x, rows, at in Y_DOWN:
        ext_a[pop, x + HX, Y0 + BY : Y0 + BY + rows, :] = above_ref[at : at + rows, :]

    own = lax.broadcasted_iota(jnp.int32, (8, BZ), 0)

    def step(source, target, margin, which):
        @pl.loop(HX - margin, HX + BX + margin)
        def _(x):
            for t in range(5):
                row = 8 + 8 * t
                f = []
                for i in range(NQ):
                    cx, cy, _ = VEL[i]
                    f.append(source[i, x - cx, pl.ds(row - cy, 8), :])
                solid = ext_a[SOLID, x, pl.ds(row, 8), :] > 0.0
                out, *sums = collide(f, solid)
                for i in range(NQ):
                    target[i, x, pl.ds(row, 8), :] = turn(out[i], i)

                at = pl.ds(pl.multiple_of(x * (BY + 8) + t * 8, 8), 8)
                for q, v in enumerate(sums):
                    if t == 0:
                        v = jnp.where(own >= 4, v, 0.0)
                    if t == 4:
                        v = jnp.where(own < 4, v, 0.0)
                    moments[which, q, at, :] = v

    step(ext_a, ext_b, 2, 0)
    step(ext_b, ext_a, 1, 1)
    step(ext_a, ext_b, 0, 2)
    n = 0
    m = 0
    for pop in range(NQ):
        cx, cy, _ = VEL[pop]
        if cx > 0:
            up_ref[n] = ext_b[pop, HX + BX - 1, 8 : 48, :]
            n += 1
        if cx < 0:
            down_ref[m] = ext_b[pop, HX, 8 : 48, :]
            m += 1
        for x in range(max(cx, 0), BX + min(cx, 0)):
            out_ref[pop, x] = ext_b[pop, x + HX - cx, Y0 - cy : Y0 - cy + BY, :]
    result = pltpu.make_async_copy(out_ref, out_hbm, sem)
    result.start()
    table = table_ref[...]
    columns = []
    for which in range(3):
        inside = pl.ds(HX * (BY + 8), BX * (BY + 8))
        sums = [moments[which, q, inside, :] for q in range(4)]
        columns += sample(sums, table, 1, BX * (BY + 8))
    put_message(lanes_of(columns), message_ref)
    result.wait()


EDGES = [(pop, 0) for pop in range(NQ) if VEL[pop][0] > 0] + [
    (pop, BX - 1) for pop in range(NQ) if VEL[pop][0] < 0
]


def last_kernel(given_ref, low_ref, high_ref, out_ref, planes, sems):
    copies = []
    for n, (pop, x) in enumerate(EDGES):
        source = low_ref.at[n] if x == 0 else high_ref.at[n - 5]
        row = 4 - VEL[pop][1]
        planes[n] = source[row : row + BY, :]
        copies.append(pltpu.make_async_copy(planes.at[n], out_ref.at[pop, x], sems.at[n]))
        copies[-1].start()
    for copy in copies:
        copy.wait()


def fit(fun, degree, odd):
    count = 400
    x = 0.25 + 0.25 * np.cos(np.pi * (np.arange(count) + 0.5) / count)
    powers = np.stack([x ** (2 * k + odd) for k in range(degree)], axis=1)
    weight = np.ones(count)
    best = None
    for _ in range(200):
        coef = np.linalg.lstsq(powers * weight[:, None], fun(x) * weight, rcond=None)[0]
        error = np.abs(powers @ coef - fun(x))
        if best is None or error.max() < best[0]:
            best = (error.max(), coef)
        weight = weight * (0.5 + error / error.max()) ** 0.5
        weight = weight / weight.max()
    return [float(c) for c in best[1]]


ROOT2 = math.sqrt(2.0)
SIN_POLY = fit(lambda x: ROOT2 * np.sin(np.pi * x), 5, 1)
COS_POLY = fit(lambda x: ROOT2 * np.cos(np.pi * x), 5, 0)


def horner(coefs, y):
    v = y * coefs[-1] + coefs[-2]
    for c in coefs[-3::-1]:
        v = v * y + c
    return v


def sin_cos_turns(t):
    x = t - jnp.round(t)
    y = x * x
    s = horner(SIN_POLY, y) * x
    c = horner(COS_POLY, y)
    return 1.0 - s * s, s * c


CHUNKS = NB * CAP // 128
TILES = 8
WIDE = 8
AHEAD = 2


def parts_of(message, alive):
    mask = jnp.concatenate(
        [jnp.broadcast_to(alive[r : r + 1, :], (NV, 2 * NB)) for r in range(8)], axis=0
    )
    return split3(jnp.where(mask > 0.0, message.T, 0.0))


def pack(parts, offset, c):
    lanes = lax.broadcasted_iota(jnp.int32, (2 * NB, 128), 1)
    hot = [
        jnp.where(offset[...] == (lanes + (c + n) * 128).astype(F32), 1.0, 0.0).astype(BF16)
        for n in (-1, 0)
    ]
    hot = jnp.concatenate(hot, axis=1)
    found = dot(parts[0], hot) + dot(parts[1], hot) + dot(parts[2], hot)
    total = found[:NV, 128:]
    for r in range(1, 8):
        total = total + pltpu.roll(found[r * NV : r * NV + NV, :], r, axis=1)[:, 128:]
    return total


def pack_by_rank(parts, places, c):
    lanes = lax.broadcasted_iota(jnp.int32, (2 * NB, 128), 1)
    here = (lanes + c * 128).astype(F32)
    total = jnp.zeros((3 * NV, 128), F32)
    for r in range(8):
        hot = jnp.where(places[r] == here, 1.0, 0.0).astype(BF16)
        total = total + dot(parts[r], hot)
    return total[:NV] + total[NV : 2 * NV] + total[2 * NV :]


def distances(obs_lanes, info, c, rows):
    d = [obs_lanes[k, rows, :] - info[c, k : k + 1, :] for k in range(3)]
    square = d[0] * d[0] + d[1] * d[1] + d[2] * d[2]
    inv = lax.rsqrt(square)
    return d, inv, square * inv


def tile_rows(o, t, tiles):
    return pl.ds(pl.multiple_of(o * 8 * tiles + 8 * t, 8), 8)


def count_of(total_ref):
    return (jnp.sum(total_ref[0:1, 0:1]).astype(jnp.int32) + 127) // 128


def table_kernel(
    freq_ref, first_ref, obs_ref, waves_hbm, offset, alive, info, obs_lanes, total_ref, places, waves, sems
):
    lane = lax.broadcasted_iota(jnp.int32, (2 * NB, 128), 1)
    first = first_ref[...]
    live = jnp.sum(jnp.where(lane % NV == 3, first, 0.0), axis=1, keepdims=True)
    lower = (
        lax.broadcasted_iota(jnp.int32, (2 * NB, 2 * NB), 0)
        > lax.broadcasted_iota(jnp.int32, (2 * NB, 2 * NB), 1)
    ).astype(F32).astype(BF16)
    live_lanes = jnp.broadcast_to(live, (2 * NB, 128))
    offset[...] = dot(lower, live_lanes.astype(BF16))
    total = jnp.sum(live)
    total_ref[...] = jnp.broadcast_to(jnp.sum(live, axis=0, keepdims=True), (8, 128))
    chunks = (total.astype(jnp.int32) + 127) // 128
    turned = first.T
    alive[...] = jnp.concatenate([turned[r * NV + 3 : r * NV + 4, :] for r in range(8)], axis=0)
    parts = []
    for r in range(8):
        places[r] = jnp.where(live_lanes > float(r), offset[...] + float(r), -1.0)
        parts.append(jnp.concatenate(split3(turned[r * NV : r * NV + NV, :]), axis=0))
    observers = obs_ref[...]
    for k in range(3):
        obs_lanes[k] = jnp.broadcast_to(observers[k : k + 1, :], (128, 256)).T
    gy = lax.axis_index("gy") * 8
    turns = [freq_ref[gy + k] * (math.sqrt(3.0) / (2.0 * math.pi)) for k in range(AHEAD)]

    def store(c):
        slot = c % 2
        return pltpu.make_async_copy(waves.at[slot], waves_hbm.at[c], sems.at[slot])

    @pl.loop(0, chunks)
    def _(c):
        info[c] = pack_by_rank(parts, places, c)
        slot = c % 2

        @pl.when(c >= 2)
        def _():
            store(c - 2).wait()

        @pl.loop(0, 32 // WIDE)
        def _(o):
            tiles = []
            for t in range(WIDE):
                rows = tile_rows(o, t, WIDE)
                _, inv, dist = distances(obs_lanes, info, c, rows)
                tiles.append((rows, inv, dist))
            for k in range(AHEAD):
                for rows, inv, dist in tiles:
                    cos, sin = sin_cos_turns(dist * turns[k])
                    waves[slot, 2 * k, rows, :] = cos * inv
                    waves[slot, 2 * k + 1, rows, :] = sin * inv

        store(c).start()

    @pl.when(chunks >= 2)
    def _():
        store(chunks - 2).wait()

    store(chunks - 1).wait()


def sum_kernel(
    freq_ref, waves_hbm, second_ref, offset, alive, info, obs_lanes, total_ref, out_ref,
    series, weights, acc, waves, sems,
):
    chunks = count_of(total_ref)

    def load(c):
        slot = c % 2
        return pltpu.make_async_copy(waves_hbm.at[c], waves.at[slot], sems.at[slot])

    load(0).start()

    @pl.when(chunks >= 2)
    def _():
        load(1).start()

    parts = parts_of(second_ref[...], alive[...])

    def packed_series(c):
        late = pack(parts, offset, c)
        fixed = info[c]
        area = [fixed[4 + k : 5 + k, :] for k in range(3)]
        keep = fixed[3:4, :]
        rows = []
        for s in range(4):
            value, at = (fixed, 7) if s == 0 else (late, 4 * (s - 1))
            rho = value[at : at + 1, :]
            j = [value[at + 1 + k : at + 2 + k, :] for k in range(3)]
            scale = 1.0 / jnp.where(keep > 0.0, rho, 1.0)
            u = [v * scale for v in j]
            flux = u[0] * area[0] + u[1] * area[1] + u[2] * area[2]
            pressure = (rho - BASE) * (1.0 / 3.0)
            rows.append(rho * flux * keep)
            for k in range(3):
                rows.append((pressure * area[k] + j[k] * flux) * keep)
        series[c] = jnp.concatenate(rows, axis=0)

    @pl.loop(0, (chunks + 1) // 2)
    def _(half):
        packed_series(2 * half)
        packed_series(2 * half + 1)

    gy = lax.axis_index("gy") * 8
    sub = lax.broadcasted_iota(jnp.int32, (8, 128), 0)
    omega = jnp.zeros((8, 128), F32)
    for k in range(8):
        omega = jnp.where(sub == k, freq_ref[gy + k], omega)
    cosines, sines = [], []
    for s in range(4):
        taper = 0.5 - 0.5 * math.cos(2.0 * math.pi * (s + 0.5) / 4)
        cosines.append(taper * jnp.cos(omega * float(s)))
        sines.append(-taper * jnp.sin(omega * float(s)))

    @pl.loop(0, chunks)
    def _(c):
        for comp in range(4):
            for part, factors in enumerate((cosines, sines)):
                v = factors[0] * series[c, comp : comp + 1, :]
                for s in range(1, 4):
                    v = v + factors[s] * series[c, 4 * s + comp : 4 * s + comp + 1, :]
                if comp == 0:
                    v = v * (1.0 / math.sqrt(3.0))
                weights[c, part * 4 + comp] = v

    turns = [freq_ref[gy + k] * (math.sqrt(3.0) / (2.0 * math.pi)) for k in range(8)]
    over_k = [1.0 / (omega[k : k + 1, :] * math.sqrt(3.0)) for k in range(8)]
    over_k = [jnp.broadcast_to(v, (8, 128)) for v in over_k]
    acc[...] = jnp.zeros_like(acc)

    @pl.loop(0, chunks)
    def _(c):
        slot = c % 2
        load(c).wait()

        @pl.loop(0, 32 // TILES)
        def _(o):
            tiles = []
            for t in range(TILES):
                rows = tile_rows(o, t, TILES)
                d, inv, dist = distances(obs_lanes, info, c, rows)
                tiles.append((rows, inv, dist, [v * inv for v in d]))
            for k in range(8):
                w = [weights[c, m, k : k + 1, :] for m in range(8)]
                for rows, inv, dist, n in tiles:
                    if k < AHEAD:
                        cos = waves[slot, 2 * k, rows, :]
                        sin = waves[slot, 2 * k + 1, rows, :]
                    else:
                        cos, sin = sin_cos_turns(dist * turns[k])
                        cos = cos * inv
                        sin = sin * inv
                    re = n[0] * w[1] + n[1] * w[2] + n[2] * w[3]
                    im = n[0] * w[5] + n[1] * w[6] + n[2] * w[7]
                    near = inv * over_k[k]
                    dr = near * re - (im + w[4])
                    di = near * im + (re + w[0])
                    acc[k, rows, :] += cos * dr + sin * di
                    acc[8 + k, rows, :] += cos * di - sin * dr

        @pl.when(c + 2 < chunks)
        def _():
            load(c + 2).start()

    lane = lax.broadcasted_iota(jnp.int32, (256, 128), 1)
    columns = jnp.zeros((256, 128), F32)
    for k in range(16):
        columns = jnp.where(lane == k, jnp.sum(acc[k], axis=1, keepdims=True), columns)
    rows = columns.T
    for k in range(16):
        wave = freq_ref[gy + k % 8] * math.sqrt(3.0)
        out_ref[k // 8, k % 8 : k % 8 + 1, :] = rows[k : k + 1, :] * wave


def call(
    kernel, shapes, scratch=(), smem=0, inputs=0, cost=1000, limit=8, far=0, alias=None, out_far=0
):
    near = pl.BlockSpec(memory_space=pltpu.VMEM)
    return pl.pallas_call(
        kernel,
        out_shape=[
            pltpu.HBM(s, F32) if n < out_far else jax.ShapeDtypeStruct(s, F32)
            for n, s in enumerate(shapes)
        ],
        in_specs=[pl.BlockSpec(memory_space=pltpu.SMEM)] * smem
        + [pl.BlockSpec(memory_space=pltpu.HBM)] * far
        + [near] * (inputs - smem - far),
        out_specs=[pl.BlockSpec(memory_space=pltpu.HBM)] * out_far + [near] * (len(shapes) - out_far),
        scratch_shapes=list(scratch),
        input_output_aliases=alias or {},
        compiler_params=pltpu.CompilerParams(vmem_limit_bytes=limit << 20),
        cost_estimate=pl.CostEstimate(flops=cost, bytes_accessed=cost, transcendentals=0),
    )


def far_away(array):
    return pltpu.with_memory_space_constraint(array, pltpu.HBM)


def ring(axis, up, down):
    count = lax.axis_size(axis)
    forward = [(i, (i + 1) % count) for i in range(count)]
    backward = [((i + 1) % count, i) for i in range(count)]
    low = lax.ppermute(up, axis, forward)
    high = lax.ppermute(down, axis, backward)
    return low, high


def exchange(message):
    return lax.all_to_all(message, ("gx", "gy"), split_axis=0, concat_axis=0, tiled=True)


def run(
    populations, solid, panel_cell, panel_owner, panel_count, panel_area, observers, frequencies
):
    cell = panel_cell.reshape(1, SLOTS)
    owner = panel_owner.reshape(1, SLOTS)
    relaxed, up, down, moments = call(
        first_kernel,
        [(NQ, BX, BY, BZ), (NXE, BY, BZ), (NXE, BY, BZ), (4, BX * BY, BZ)],
        [
            pltpu.VMEM((NQ, BX, BY, BZ), F32),
            pltpu.VMEM((BX, BY, BZ), jnp.int32),
            pltpu.SemaphoreType.DMA((BX + 1,)),
        ],
        inputs=2,
        far=2,
        limit=12,
    )(far_away(populations), far_away(solid))
    table, message_a = call(
        slots_kernel, [(SLOTS, 128), (2 * NB, 128)], smem=1, inputs=5
    )(panel_count, cell, owner, panel_area, moments)
    low, high = ring("gx", up, down)
    y_up, y_down = call(edge_kernel, [(NYE, BZ)] * 2, inputs=4)(relaxed, solid, low, high)
    below, above = ring("gy", y_up, y_down)
    got_a = exchange(message_a)
    current, up, down, message_b = call(
        steps_kernel,
        [(NQ, BX, BY, BZ), (5, BY + 8, BZ), (5, BY + 8, BZ), (2 * NB, 128)],
        [
            pltpu.VMEM((NQ + 1, BX + 2 * HX, YR, BZ), F32),
            pltpu.VMEM((NQ, BX + 2 * HX, YR, BZ), F32),
            pltpu.VMEM((3, 4, (BX + 2 * HX) * (BY + 8), BZ), F32),
            pltpu.VMEM((NQ, BX, BY, BZ), F32),
            pltpu.SemaphoreType.DMA,
        ],
        out_far=1,
        inputs=7,
        limit=28,
    )(relaxed, solid, low, high, below, above, table)
    got_b = exchange(message_b)
    low, high = ring("gx", up, down)
    (current,) = call(
        last_kernel,
        [(NQ, BX, BY, BZ)],
        [pltpu.VMEM((len(EDGES), BY, BZ), F32), pltpu.SemaphoreType.DMA((len(EDGES),))],
        inputs=3,
        far=1,
        out_far=1,
        alias={0: 0},
        limit=4,
    )(current, low, high)
    waves, *tables = call(
        table_kernel,
        [
            (CHUNKS, 2 * AHEAD, 256, 128),
            (2 * NB, 128),
            (8, 2 * NB),
            (CHUNKS, NV, 128),
            (3, 256, 128),
            (8, 128),
        ],
        [
            pltpu.VMEM((8, 2 * NB, 128), F32),
            pltpu.VMEM((2, 2 * AHEAD, 256, 128), F32),
            pltpu.SemaphoreType.DMA((2,)),
        ],
        out_far=1,
        smem=1,
        inputs=3,
        limit=6,
    )(frequencies, got_a, observers)
    (spectra,) = call(
        sum_kernel,
        [(2, 8, 256)],
        [
            pltpu.VMEM((CHUNKS, 16, 128), F32),
            pltpu.VMEM((CHUNKS, 8, 8, 128), F32),
            pltpu.VMEM((16, 256, 128), F32),
            pltpu.VMEM((2, 2 * AHEAD, 256, 128), F32),
            pltpu.SemaphoreType.DMA((2,)),
        ],
        smem=1,
        far=1,
        inputs=8,
        limit=10,
    )(frequencies, far_away(waves), got_b, *tables)
    return current, spectra[None]


def solution(mesh):
    return jax.shard_map(
        run,
        mesh=mesh,
        in_specs=(
            P(None, "gx", "gy", None),
            P("gx", "gy", None),
            P(("gx", "gy")),
            P(("gx", "gy")),
            P(("gx", "gy")),
            P(None, ("gx", "gy")),
            P(),
            P(),
        ),
        out_specs=(P(None, "gx", "gy", None), P("gx", None, "gy", None)),
        check_vma=False,
    )
```

```python
import math

import jax
import jax.numpy as jnp
import numpy as np
from jax import lax
from jax.experimental import pallas as pl
from jax.experimental.pallas import tpu as pltpu
from jax.sharding import PartitionSpec as P


F32 = jnp.float32
BF16 = jnp.bfloat16

VEL = [
    (0, 0, 0), (1, 0, 0), (-1, 0, 0), (0, 1, 0), (0, -1, 0), (0, 0, 1), (0, 0, -1),
    (1, 1, 0), (-1, -1, 0), (1, -1, 0), (-1, 1, 0), (1, 0, 1), (-1, 0, -1),
    (1, 0, -1), (-1, 0, 1), (0, 1, 1), (0, -1, -1), (0, 1, -1), (0, -1, 1),
]
NQ = 19
BX, BY, BZ = 4, 32, 128
SOLID = 19
HX = 3
Y0 = 12
YR = 56
SLOTS = 256
PATCH = 16
CAP = 16
NB = 128
NV = 16
BASE = 19.0


def x_entries(side):
    out = []
    for dist in (1, 2, 3):
        for pop in range(NQ):
            along = VEL[pop][0] * side
            if dist == 1 or (dist == 2 and along >= 0) or (dist == 3 and along > 0):
                out.append((pop, dist))
        if dist < 3:
            out.append((SOLID, dist))
    return out


X_UP = x_entries(1)
X_DOWN = x_entries(-1)
NXE = len(X_UP)


def y_entries(side):
    out, at = [], 0
    for x in range(-HX, BX + HX):
        far = -x if x < 0 else (x - BX + 1 if x >= BX else 0)
        inward = 1 if x < 0 else -1
        for pop in range(NQ + 1):
            if pop == SOLID:
                if far > 2:
                    continue
                rows = 3
            else:
                along = VEL[pop][0] * inward
                if (far == 2 and along < 0) or (far == 3 and along <= 0):
                    continue
                rows = 3 + VEL[pop][1] * side
            out.append((pop, x, rows, at))
            at += rows
    return out, at


Y_UP, NYE = y_entries(1)
Y_DOWN, NYE_DOWN = y_entries(-1)
assert NYE == NYE_DOWN


def collide(f, solid):
    pair = [f[i] + f[i + 1] for i in range(1, NQ, 2)]
    diff = [f[i] - f[i + 1] for i in range(1, NQ, 2)]
    px, py, pz, pa, pb, pc, pd, pe, pf = pair
    dx, dy, dz, da, db, dc, dd, de, df = diff
    sxy, sxz, syz = pa + pb, pc + pd, pe + pf
    qxy, qxz, qyz = pa - pb, pc - pd, pe - pf
    rho = (f[0] + px) + (py + pz) + (sxy + (sxz + syz))
    jx = dx + (da + db) + (dc + dd)
    jy = dy + (da - db) + (de + df)
    jz = dz + (dc - dd) + (de - df)
    inv = 1.0 / rho
    ux, uy, uz = jx * inv, jy * inv, jz * inv
    exx, eyy, ezz = jx * ux, jy * uy, jz * uz
    exy, exz, eyz = jx * uy, jx * uz, jy * uz
    base = rho - 1.5 * (exx + eyy + ezz)
    third = rho * (1.0 / 3.0)
    bx = (px + sxy + sxz) - third - exx
    by = (py + sxy + syz) - third - eyy
    bz = (pz + sxz + syz) - third - ezz
    trace = bx + by + bz
    out = [None] * NQ
    out[0] = -0.2 * f[0] + 0.4 * base + trace * (1.0 / 7.0)
    axis_common = base * (0.6 / 9.0) + trace * (0.6 / 7.0)
    diag_common = base * (0.6 / 18.0) + trace * (0.2 / 7.0)
    ax = [0.3 * e - 0.1 * b for e, b in ((exx, bx), (eyy, by), (ezz, bz))]
    dg = [0.15 * e - 0.1 * b for e, b in ((exx, bx), (eyy, by), (ezz, bz))]
    half = [axis_common + a - 0.1 * p for a, p in zip(ax, (px, py, pz))]
    for (i, k), e, q, (p1, p2) in (
        ((0, 1), exy, qxy, (pa, pb)),
        ((0, 2), exz, qxz, (pc, pd)),
        ((1, 2), eyz, qyz, (pe, pf)),
    ):
        common = diag_common + (dg[i] + dg[k])
        twist = 0.3 * e - 0.15 * (q - e)
        half.append(common + twist - 0.1 * p1)
        half.append(common - twist - 0.1 * p2)
    a, b = 0.7 / 3.0, 0.7 / 6.0
    flow = [jx * a, jy * a, jz * a]
    kx, ky, kz = jx * b, jy * b, jz * b
    flow += [kx + ky, kx - ky, kx + kz, kx - kz, ky + kz, ky - kz]
    for n in range(9):
        odd = flow[n] - 0.2 * diff[n]
        out[2 * n + 1] = half[n] + odd
        out[2 * n + 2] = half[n] - odd
    opposite = [0] + [i + 1 if i % 2 else i - 1 for i in range(1, NQ)]
    out = [jnp.where(solid, f[opposite[i]], out[i]) for i in range(NQ)]
    return out, rho, jx, jy, jz


def split3(v):
    hi = v.astype(BF16)
    rest = v - hi.astype(F32)
    mid = rest.astype(BF16)
    lo = (rest - mid.astype(F32)).astype(BF16)
    return hi, mid, lo


def dot(a, b):
    return jnp.dot(a, b, preferred_element_type=F32)


def sample(moments, table, column, rows):
    row_hot = (
        lax.broadcasted_iota(jnp.int32, (SLOTS, rows), 1).astype(F32) == table[:, column : column + 1]
    ).astype(F32).astype(BF16)
    row_hot = jnp.concatenate([row_hot] * 3, axis=1)
    lane = lax.broadcasted_iota(jnp.int32, (SLOTS, BZ), 1).astype(F32)
    z_hot = lane == table[:, 2:3]
    columns = []
    for q in range(4):
        got = dot(row_hot, jnp.concatenate(split3(moments[q]), axis=0))
        columns.append(jnp.sum(jnp.where(z_hot, got, 0.0), axis=1, keepdims=True))
    return columns


def put_message(values, out_ref):
    halves = []
    for part in range(2):
        total = jnp.zeros((PATCH, 128), F32)
        for r in range(8):
            at = (part * 8 + r) * PATCH
            block = values[at : at + PATCH, :]
            total = total + (pltpu.roll(block, r * NV, axis=1) if r else block)
        halves.append(total)
    odd = lax.broadcasted_iota(jnp.int32, (16, 128), 0) % 2 == 1
    for p in range(PATCH):
        out_ref[p * 16 : p * 16 + 16, :] = jnp.where(
            odd,
            jnp.broadcast_to(halves[1][p : p + 1, :], (16, 128)),
            jnp.broadcast_to(halves[0][p : p + 1, :], (16, 128)),
        )


def lanes_of(columns, start=0):
    lane = lax.broadcasted_iota(jnp.int32, (SLOTS, 128), 1)
    out = jnp.zeros((SLOTS, 128), F32)
    for i, column in enumerate(columns):
        out = jnp.where(lane == start + i, column, out)
    return out


def turn(v, pop):
    step = VEL[pop][2]
    return pltpu.roll(v, step % BZ, axis=1) if step else v


def first_kernel(f_hbm, solid_hbm, relaxed_ref, up_ref, down_ref, moments_ref, f_ref, solid_ref, sems):
    def plane(x):
        return pltpu.make_async_copy(f_hbm.at[:, x], f_ref.at[:, x], sems.at[x])

    mask = pltpu.make_async_copy(solid_hbm, solid_ref, sems.at[BX])
    mask.start()
    for x in range(BX):
        plane(x).start()
    mask.wait()

    @pl.loop(0, BX)
    def _(x):
        plane(x).wait()
        for t in range(BY // 8):
            rows = pl.ds(t * 8, 8)
            f = [f_ref[i, x, rows, :] for i in range(NQ)]
            out, *sums = collide(f, solid_ref[x, rows, :] > 0)
            for i in range(NQ):
                relaxed_ref[i, x, rows, :] = turn(out[i], i)
            at = pl.ds(pl.multiple_of(x * BY + t * 8, 8), 8)
            for q, v in enumerate(sums):
                moments_ref[q, at, :] = v

    for n, (pop, dist) in enumerate(X_UP):
        x = BX - dist
        up_ref[n] = solid_ref[x].astype(F32) if pop == SOLID else relaxed_ref[pop, x]
    for n, (pop, dist) in enumerate(X_DOWN):
        x = dist - 1
        down_ref[n] = solid_ref[x].astype(F32) if pop == SOLID else relaxed_ref[pop, x]


def slots_kernel(count_ref, cell_ref, owner_ref, area_ref, moments_ref, table_ref, message_ref):
    cell = cell_ref[...]
    owner = owner_ref[...].astype(F32)
    local_x = cell // (BY * BZ)
    local_y = (cell // BZ) % BY
    local_z = cell % BZ
    slot = lax.broadcasted_iota(jnp.int32, (1, SLOTS), 1)
    live = (slot < count_ref[0]).astype(F32)
    gx = (lax.axis_index("gx") * BX).astype(jnp.int32)
    gy = (lax.axis_index("gy") * BY).astype(jnp.int32)
    across = jnp.broadcast_to(owner, (SLOTS, SLOTS))
    same = across.T == across
    earlier = lax.broadcasted_iota(jnp.int32, (SLOTS, SLOTS), 0) < lax.broadcasted_iota(
        jnp.int32, (SLOTS, SLOTS), 1
    )
    rank = jnp.sum(jnp.where(same & earlier, 1.0, 0.0), axis=0, keepdims=True)
    place = rank * PATCH + owner
    order = (
        lax.broadcasted_iota(jnp.int32, (SLOTS, SLOTS), 0).astype(F32)
        == jnp.broadcast_to(place, (SLOTS, SLOTS))
    ).astype(F32).astype(BF16)
    exact = [
        (local_x * BY + local_y).astype(F32),
        (local_x * (BY + 8) + local_y + 4).astype(F32),
        local_z.astype(F32),
        (local_x + gx).astype(F32),
        (local_y + gy).astype(F32),
        live,
    ]
    pad = jnp.zeros((1, SLOTS), F32)
    area = area_ref[...]
    hi, mid, lo = split3(jnp.concatenate([area, jnp.zeros((5, SLOTS), F32)], axis=0))
    first = jnp.concatenate(exact + [pad, pad], axis=0).astype(BF16)
    source = jnp.concatenate(
        [v.astype(F32) for v in (first, hi, mid, lo)] + [jnp.zeros((96, SLOTS), F32)], axis=0
    ).astype(BF16)
    raw = lax.dot_general(order, source, (((1,), (1,)), ((), ())), preferred_element_type=F32)
    area_cols = [
        raw[:, 8 + k : 9 + k] + raw[:, 16 + k : 17 + k] + raw[:, 24 + k : 25 + k] for k in range(3)
    ]
    table_ref[...] = raw
    picked = sample([moments_ref[q] for q in range(4)], raw, 0, BX * BY)
    fixed = [raw[:, 3:4], raw[:, 4:5], raw[:, 2:3], raw[:, 5:6]] + area_cols
    put_message(lanes_of(fixed + picked), message_ref)


def edge_kernel(relaxed_ref, solid_ref, low_ref, high_ref, up_ref, down_ref):
    low = {(pop, -dist): n for n, (pop, dist) in enumerate(X_UP)}
    high = {(pop, BX - 1 + dist): n for n, (pop, dist) in enumerate(X_DOWN)}

    def rows_of(pop, x, start, count):
        if x < 0:
            return low_ref[low[pop, x], start : start + count, :]
        if x >= BX:
            return high_ref[high[pop, x], start : start + count, :]
        if pop == SOLID:
            return solid_ref[x, start : start + count, :].astype(F32)
        return relaxed_ref[pop, x, start : start + count, :]

    for pop, x, rows, at in Y_UP:
        up_ref[at : at + rows, :] = rows_of(pop, x, BY - rows, rows)
    for pop, x, rows, at in Y_DOWN:
        down_ref[at : at + rows, :] = rows_of(pop, x, 0, rows)


def steps_kernel(
    relaxed_ref, solid_ref, low_ref, high_ref, below_ref, above_ref, table_ref,
    out_hbm, up_ref, down_ref, message_ref, ext_a, ext_b, moments, out_ref, sem,
):
    for x in range(BX):
        for pop in range(NQ):
            ext_a[pop, x + HX, Y0 : Y0 + BY, :] = relaxed_ref[pop, x]
        ext_a[SOLID, x + HX, Y0 : Y0 + BY, :] = solid_ref[x].astype(F32)
    for n, (pop, dist) in enumerate(X_UP):
        ext_a[pop, HX - dist, Y0 : Y0 + BY, :] = low_ref[n]
    for n, (pop, dist) in enumerate(X_DOWN):
        ext_a[pop, HX + BX - 1 + dist, Y0 : Y0 + BY, :] = high_ref[n]
    for pop, x, rows, at in Y_UP:
        ext_a[pop, x + HX, Y0 - rows : Y0, :] = below_ref[at : at + rows, :]
    for pop, x, rows, at in Y_DOWN:
        ext_a[pop, x + HX, Y0 + BY : Y0 + BY + rows, :] = above_ref[at : at + rows, :]

    own = lax.broadcasted_iota(jnp.int32, (8, BZ), 0)

    def step(source, target, margin, which):
        @pl.loop(HX - margin, HX + BX + margin, unroll=2)
        def _(x):
            for t in range(5):
                row = 8 + 8 * t
                f = []
                for i in range(NQ):
                    cx, cy, _ = VEL[i]
                    f.append(source[i, x - cx, pl.ds(row - cy, 8), :])
                solid = ext_a[SOLID, x, pl.ds(row, 8), :] > 0.0
                out, *sums = collide(f, solid)
                for i in range(NQ):
                    target[i, x, pl.ds(row, 8), :] = turn(out[i], i)

                at = pl.ds(pl.multiple_of(x * (BY + 8) + t * 8, 8), 8)
                for q, v in enumerate(sums):
                    if t == 0:
                        v = jnp.where(own >= 4, v, 0.0)
                    if t == 4:
                        v = jnp.where(own < 4, v, 0.0)
                    moments[which, q, at, :] = v

    step(ext_a, ext_b, 2, 0)
    step(ext_b, ext_a, 1, 1)
    step(ext_a, ext_b, 0, 2)
    n = 0
    m = 0
    for pop in range(NQ):
        cx, cy, _ = VEL[pop]
        if cx > 0:
            up_ref[n] = ext_b[pop, HX + BX - 1, 8 : 48, :]
            n += 1
        if cx < 0:
            down_ref[m] = ext_b[pop, HX, 8 : 48, :]
            m += 1
        for x in range(max(cx, 0), BX + min(cx, 0)):
            out_ref[pop, x] = ext_b[pop, x + HX - cx, Y0 - cy : Y0 - cy + BY, :]
    result = pltpu.make_async_copy(out_ref, out_hbm, sem)
    result.start()
    table = table_ref[...]
    columns = []
    for which in range(3):
        inside = pl.ds(HX * (BY + 8), BX * (BY + 8))
        sums = [moments[which, q, inside, :] for q in range(4)]
        columns += sample(sums, table, 1, BX * (BY + 8))
    put_message(lanes_of(columns), message_ref)
    result.wait()


EDGES = [(pop, 0) for pop in range(NQ) if VEL[pop][0] > 0] + [
    (pop, BX - 1) for pop in range(NQ) if VEL[pop][0] < 0
]


def last_kernel(given_ref, low_ref, high_ref, out_ref, planes, sems):
    copies = []
    for n, (pop, x) in enumerate(EDGES):
        source = low_ref.at[n] if x == 0 else high_ref.at[n - 5]
        row = 4 - VEL[pop][1]
        planes[n] = source[row : row + BY, :]
        copies.append(pltpu.make_async_copy(planes.at[n], out_ref.at[pop, x], sems.at[n]))
        copies[-1].start()
    for copy in copies:
        copy.wait()


def fit(fun, degree, odd):
    count = 400
    x = 0.25 + 0.25 * np.cos(np.pi * (np.arange(count) + 0.5) / count)
    powers = np.stack([x ** (2 * k + odd) for k in range(degree)], axis=1)
    weight = np.ones(count)
    best = None
    for _ in range(200):
        coef = np.linalg.lstsq(powers * weight[:, None], fun(x) * weight, rcond=None)[0]
        error = np.abs(powers @ coef - fun(x))
        if best is None or error.max() < best[0]:
            best = (error.max(), coef)
        weight = weight * (0.5 + error / error.max()) ** 0.5
        weight = weight / weight.max()
    return [float(c) for c in best[1]]


ROOT2 = math.sqrt(2.0)
SIN_POLY = fit(lambda x: ROOT2 * np.sin(np.pi * x), 5, 1)
COS_POLY = fit(lambda x: ROOT2 * np.cos(np.pi * x), 5, 0)


def horner(coefs, y):
    v = y * coefs[-1] + coefs[-2]
    for c in coefs[-3::-1]:
        v = v * y + c
    return v


def sin_cos_turns(t):
    x = t - jnp.round(t)
    y = x * x
    s = horner(SIN_POLY, y) * x
    c = horner(COS_POLY, y)
    return 1.0 - s * s, s * c


CHUNKS = NB * CAP // 128
TILES = 4
WIDE = 4
AHEAD = 2


def parts_of(message, alive):
    mask = jnp.concatenate(
        [jnp.broadcast_to(alive[r : r + 1, :], (NV, 2 * NB)) for r in range(8)], axis=0
    )
    return split3(jnp.where(mask > 0.0, message.T, 0.0))


def pack(parts, offset, c):
    lanes = lax.broadcasted_iota(jnp.int32, (2 * NB, 128), 1)
    hot = [
        jnp.where(offset[...] == (lanes + (c + n) * 128).astype(F32), 1.0, 0.0).astype(BF16)
        for n in (-1, 0)
    ]
    hot = jnp.concatenate(hot, axis=1)
    found = dot(parts[0], hot) + dot(parts[1], hot) + dot(parts[2], hot)
    total = found[:NV, 128:]
    for r in range(1, 8):
        total = total + pltpu.roll(found[r * NV : r * NV + NV, :], r, axis=1)[:, 128:]
    return total


def pack_by_rank(parts, places, c):
    lanes = lax.broadcasted_iota(jnp.int32, (2 * NB, 128), 1)
    here = (lanes + c * 128).astype(F32)
    total = jnp.zeros((3 * NV, 128), F32)
    for r in range(8):
        hot = jnp.where(places[r] == here, 1.0, 0.0).astype(BF16)
        total = total + dot(parts[r], hot)
    return total[:NV] + total[NV : 2 * NV] + total[2 * NV :]


def distances(obs_lanes, info, c, rows):
    d = [obs_lanes[k, rows, :] - info[c, k : k + 1, :] for k in range(3)]
    square = d[0] * d[0] + d[1] * d[1] + d[2] * d[2]
    inv = lax.rsqrt(square)
    return d, inv, square * inv


def tile_rows(o, t, tiles):
    return pl.ds(pl.multiple_of(o * 8 * tiles + 8 * t, 8), 8)


def count_of(total_ref):
    return (jnp.sum(total_ref[0:1, 0:1]).astype(jnp.int32) + 127) // 128


def table_kernel(
    freq_ref, first_ref, obs_ref, waves_hbm, offset, alive, info, obs_lanes, total_ref, places, waves, sems
):
    lane = lax.broadcasted_iota(jnp.int32, (2 * NB, 128), 1)
    first = first_ref[...]
    live = jnp.sum(jnp.where(lane % NV == 3, first, 0.0), axis=1, keepdims=True)
    lower = (
        lax.broadcasted_iota(jnp.int32, (2 * NB, 2 * NB), 0)
        > lax.broadcasted_iota(jnp.int32, (2 * NB, 2 * NB), 1)
    ).astype(F32).astype(BF16)
    live_lanes = jnp.broadcast_to(live, (2 * NB, 128))
    offset[...] = dot(lower, live_lanes.astype(BF16))
    total = jnp.sum(live)
    total_ref[...] = jnp.broadcast_to(jnp.sum(live, axis=0, keepdims=True), (8, 128))
    chunks = (total.astype(jnp.int32) + 127) // 128
    turned = first.T
    alive[...] = jnp.concatenate([turned[r * NV + 3 : r * NV + 4, :] for r in range(8)], axis=0)
    parts = []
    for r in range(8):
        places[r] = jnp.where(live_lanes > float(r), offset[...] + float(r), -1.0)
        parts.append(jnp.concatenate(split3(turned[r * NV : r * NV + NV, :]), axis=0))
    observers = obs_ref[...]
    for k in range(3):
        obs_lanes[k] = jnp.broadcast_to(observers[k : k + 1, :], (128, 256)).T
    gy = lax.axis_index("gy") * 8
    turns = [freq_ref[gy + k] * (math.sqrt(3.0) / (2.0 * math.pi)) for k in range(AHEAD)]

    def store(c):
        slot = c % 2
        return pltpu.make_async_copy(waves.at[slot], waves_hbm.at[c], sems.at[slot])

    @pl.loop(0, chunks)
    def _(c):
        info[c] = pack_by_rank(parts, places, c)
        slot = c % 2

        @pl.when(c >= 2)
        def _():
            store(c - 2).wait()

        @pl.loop(0, 32 // WIDE)
        def _(o):
            tiles = []
            for t in range(WIDE):
                rows = tile_rows(o, t, WIDE)
                _, inv, dist = distances(obs_lanes, info, c, rows)
                tiles.append((rows, inv, dist))
            for k in range(AHEAD):
                for rows, inv, dist in tiles:
                    cos, sin = sin_cos_turns(dist * turns[k])
                    waves[slot, 2 * k, rows, :] = cos * inv
                    waves[slot, 2 * k + 1, rows, :] = sin * inv

        store(c).start()

    @pl.when(chunks >= 2)
    def _():
        store(chunks - 2).wait()

    store(chunks - 1).wait()


def sum_kernel(
    freq_ref, waves_hbm, second_ref, offset, alive, info, obs_lanes, total_ref, out_ref,
    series, weights, acc, waves, sems,
):
    chunks = count_of(total_ref)

    def load(c):
        slot = c % 2
        return pltpu.make_async_copy(waves_hbm.at[c], waves.at[slot], sems.at[slot])

    load(0).start()

    @pl.when(chunks >= 2)
    def _():
        load(1).start()

    parts = parts_of(second_ref[...], alive[...])

    def packed_series(c):
        late = pack(parts, offset, c)
        fixed = info[c]
        area = [fixed[4 + k : 5 + k, :] for k in range(3)]
        keep = fixed[3:4, :]
        rows = []
        for s in range(4):
            value, at = (fixed, 7) if s == 0 else (late, 4 * (s - 1))
            rho = value[at : at + 1, :]
            j = [value[at + 1 + k : at + 2 + k, :] for k in range(3)]
            scale = 1.0 / jnp.where(keep > 0.0, rho, 1.0)
            u = [v * scale for v in j]
            flux = u[0] * area[0] + u[1] * area[1] + u[2] * area[2]
            pressure = (rho - BASE) * (1.0 / 3.0)
            rows.append(rho * flux * keep)
            for k in range(3):
                rows.append((pressure * area[k] + j[k] * flux) * keep)
        series[c] = jnp.concatenate(rows, axis=0)

    @pl.loop(0, (chunks + 1) // 2)
    def _(half):
        packed_series(2 * half)
        packed_series(2 * half + 1)

    gy = lax.axis_index("gy") * 8
    sub = lax.broadcasted_iota(jnp.int32, (8, 128), 0)
    omega = jnp.zeros((8, 128), F32)
    for k in range(8):
        omega = jnp.where(sub == k, freq_ref[gy + k], omega)
    cosines, sines = [], []
    for s in range(4):
        taper = 0.5 - 0.5 * math.cos(2.0 * math.pi * (s + 0.5) / 4)
        cosines.append(taper * jnp.cos(omega * float(s)))
        sines.append(-taper * jnp.sin(omega * float(s)))

    @pl.loop(0, chunks)
    def _(c):
        for comp in range(4):
            for part, factors in enumerate((cosines, sines)):
                v = factors[0] * series[c, comp : comp + 1, :]
                for s in range(1, 4):
                    v = v + factors[s] * series[c, 4 * s + comp : 4 * s + comp + 1, :]
                if comp == 0:
                    v = v * (1.0 / math.sqrt(3.0))
                weights[c, part * 4 + comp] = v

    turns = [freq_ref[gy + k] * (math.sqrt(3.0) / (2.0 * math.pi)) for k in range(8)]
    over_k = [1.0 / (omega[k : k + 1, :] * math.sqrt(3.0)) for k in range(8)]
    over_k = [jnp.broadcast_to(v, (8, 128)) for v in over_k]
    acc[...] = jnp.zeros_like(acc)

    @pl.loop(0, chunks)
    def _(c):
        slot = c % 2
        load(c).wait()

        @pl.loop(0, 32 // TILES)
        def _(o):
            tiles = []
            for t in range(TILES):
                rows = tile_rows(o, t, TILES)
                d, inv, dist = distances(obs_lanes, info, c, rows)
                tiles.append((rows, inv, dist, [v * inv for v in d]))
            for k in range(8):
                w = [weights[c, m, k : k + 1, :] for m in range(8)]
                for rows, inv, dist, n in tiles:
                    if k < AHEAD:
                        cos = waves[slot, 2 * k, rows, :]
                        sin = waves[slot, 2 * k + 1, rows, :]
                    else:
                        cos, sin = sin_cos_turns(dist * turns[k])
                        cos = cos * inv
                        sin = sin * inv
                    re = n[0] * w[1] + n[1] * w[2] + n[2] * w[3]
                    im = n[0] * w[5] + n[1] * w[6] + n[2] * w[7]
                    near = inv * over_k[k]
                    dr = near * re - (im + w[4])
                    di = near * im + (re + w[0])
                    acc[k, rows, :] += cos * dr + sin * di
                    acc[8 + k, rows, :] += cos * di - sin * dr

        @pl.when(c + 2 < chunks)
        def _():
            load(c + 2).start()

    lane = lax.broadcasted_iota(jnp.int32, (256, 128), 1)
    columns = jnp.zeros((256, 128), F32)
    for k in range(16):
        columns = jnp.where(lane == k, jnp.sum(acc[k], axis=1, keepdims=True), columns)
    rows = columns.T
    for k in range(16):
        wave = freq_ref[gy + k % 8] * math.sqrt(3.0)
        out_ref[k // 8, k % 8 : k % 8 + 1, :] = rows[k : k + 1, :] * wave


def call(
    kernel, shapes, scratch=(), smem=0, inputs=0, cost=1000, limit=8, far=0, alias=None, out_far=0
):
    near = pl.BlockSpec(memory_space=pltpu.VMEM)
    return pl.pallas_call(
        kernel,
        out_shape=[
            pltpu.HBM(s, F32) if n < out_far else jax.ShapeDtypeStruct(s, F32)
            for n, s in enumerate(shapes)
        ],
        in_specs=[pl.BlockSpec(memory_space=pltpu.SMEM)] * smem
        + [pl.BlockSpec(memory_space=pltpu.HBM)] * far
        + [near] * (inputs - smem - far),
        out_specs=[pl.BlockSpec(memory_space=pltpu.HBM)] * out_far + [near] * (len(shapes) - out_far),
        scratch_shapes=list(scratch),
        input_output_aliases=alias or {},
        compiler_params=pltpu.CompilerParams(vmem_limit_bytes=limit << 20),
        cost_estimate=pl.CostEstimate(flops=cost, bytes_accessed=cost, transcendentals=0),
    )


def far_away(array):
    return pltpu.with_memory_space_constraint(array, pltpu.HBM)


def ring(axis, up, down):
    count = lax.axis_size(axis)
    forward = [(i, (i + 1) % count) for i in range(count)]
    backward = [((i + 1) % count, i) for i in range(count)]
    low = lax.ppermute(up, axis, forward)
    high = lax.ppermute(down, axis, backward)
    return low, high


def exchange(message):
    return lax.all_to_all(message, ("gx", "gy"), split_axis=0, concat_axis=0, tiled=True)


def run(
    populations, solid, panel_cell, panel_owner, panel_count, panel_area, observers, frequencies
):
    cell = panel_cell.reshape(1, SLOTS)
    owner = panel_owner.reshape(1, SLOTS)
    relaxed, up, down, moments = call(
        first_kernel,
        [(NQ, BX, BY, BZ), (NXE, BY, BZ), (NXE, BY, BZ), (4, BX * BY, BZ)],
        [
            pltpu.VMEM((NQ, BX, BY, BZ), F32),
            pltpu.VMEM((BX, BY, BZ), jnp.int32),
            pltpu.SemaphoreType.DMA((BX + 1,)),
        ],
        inputs=2,
        far=2,
        limit=12,
    )(far_away(populations), far_away(solid))
    table, message_a = call(
        slots_kernel, [(SLOTS, 128), (2 * NB, 128)], smem=1, inputs=5
    )(panel_count, cell, owner, panel_area, moments)
    low, high = ring("gx", up, down)
    y_up, y_down = call(edge_kernel, [(NYE, BZ)] * 2, inputs=4)(relaxed, solid, low, high)
    below, above = ring("gy", y_up, y_down)
    got_a = exchange(message_a)
    current, up, down, message_b = call(
        steps_kernel,
        [(NQ, BX, BY, BZ), (5, BY + 8, BZ), (5, BY + 8, BZ), (2 * NB, 128)],
        [
            pltpu.VMEM((NQ + 1, BX + 2 * HX, YR, BZ), F32),
            pltpu.VMEM((NQ, BX + 2 * HX, YR, BZ), F32),
            pltpu.VMEM((3, 4, (BX + 2 * HX) * (BY + 8), BZ), F32),
            pltpu.VMEM((NQ, BX, BY, BZ), F32),
            pltpu.SemaphoreType.DMA,
        ],
        out_far=1,
        inputs=7,
        limit=28,
    )(relaxed, solid, low, high, below, above, table)
    got_b = exchange(message_b)
    low, high = ring("gx", up, down)
    (current,) = call(
        last_kernel,
        [(NQ, BX, BY, BZ)],
        [pltpu.VMEM((len(EDGES), BY, BZ), F32), pltpu.SemaphoreType.DMA((len(EDGES),))],
        inputs=3,
        far=1,
        out_far=1,
        alias={0: 0},
        limit=4,
    )(current, low, high)
    waves, *tables = call(
        table_kernel,
        [
            (CHUNKS, 2 * AHEAD, 256, 128),
            (2 * NB, 128),
            (8, 2 * NB),
            (CHUNKS, NV, 128),
            (3, 256, 128),
            (8, 128),
        ],
        [
            pltpu.VMEM((8, 2 * NB, 128), F32),
            pltpu.VMEM((2, 2 * AHEAD, 256, 128), F32),
            pltpu.SemaphoreType.DMA((2,)),
        ],
        out_far=1,
        smem=1,
        inputs=3,
        limit=6,
    )(frequencies, got_a, observers)
    (spectra,) = call(
        sum_kernel,
        [(2, 8, 256)],
        [
            pltpu.VMEM((CHUNKS, 16, 128), F32),
            pltpu.VMEM((CHUNKS, 8, 8, 128), F32),
            pltpu.VMEM((16, 256, 128), F32),
            pltpu.VMEM((2, 2 * AHEAD, 256, 128), F32),
            pltpu.SemaphoreType.DMA((2,)),
        ],
        smem=1,
        far=1,
        inputs=8,
        limit=10,
    )(frequencies, far_away(waves), got_b, *tables)
    return current, spectra[None]


def solution(mesh):
    return jax.shard_map(
        run,
        mesh=mesh,
        in_specs=(
            P(None, "gx", "gy", None),
            P("gx", "gy", None),
            P(("gx", "gy")),
            P(("gx", "gy")),
            P(("gx", "gy")),
            P(None, ("gx", "gy")),
            P(),
            P(),
        ),
        out_specs=(P(None, "gx", "gy", None), P("gx", None, "gy", None)),
        check_vma=False,
    )
```
